256 devices in a mesh: rep: 2 (over core), seq: 16 (over z, y_hi), head: 8 (over y_lo, x).
Axes of the slice: x: 4, y: 4 (y_hi: 2, y_lo: 2; y = y_hi * 2 + y_lo), z: 8, core: 2. Of those that a mesh axis runs over, the one named last changes fastest.
Arguments:
- query_latent: bfloat16 [2, 2048, 1536], P('rep', 'seq'), may hold values from -72 to 72
- kv_latent: bfloat16 [2, 2048, 576], P('rep', 'seq'), may hold values from -72 to 72
- query_up: bfloat16 [1536, 12288], P(None, 'head'), may hold values from -0.15625 to 0.15625
- kv_up: bfloat16 [512, 16384], P(None, 'head'), may hold values from -0.25 to 0.25
- out_grad: bfloat16 [2, 2048, 8192], P('rep', 'seq', 'head'), may hold values from -6 to 6
- positions: int32 [2, 2048], P('rep'), may hold values from 0 to 1535, as said below
Outputs:
- query_grad: bfloat16 [2, 2048, 1536], P('rep', 'seq')
- latent_grad: bfloat16 [2, 2048, 576], P('rep', ('seq', 'head'))
- query_up_grad: bfloat16 [1536, 12288], P(('rep', 'seq'), 'head')
The draws below stay inside these ranges and needn't reach their ends.
Inputs may be any that keep to these rules, and one draw needn't show every extreme that they name: In each window, positions count tokens from the start of their document, rising by one a token and restarting at 0 where a document begins; a window's first token has position 0; the first document is exactly 1536 tokens long and no document is longer.
All inputs are finite; a program needn't handle non-finite values.
Results may differ from the reference program's by a relative error of at most 0.013.
The reference program's roundings to bfloat16 on the way (of `queries`, `score_grad` and `head_query_grad`) count: a program that leaves them out, or rounds other values in their place, can miss the bound.
Values may be sent and summed in bfloat16 or wider, within the bound.
A program may use at most 128 MiB of HBM per device.

```python
import jax
import jax.numpy as jnp
from jax import lax

QL = 1536
KVL = 512
ROPE = 64
NOPE = 128
VD = 128
H = 64
TOKENS = 2048
WINDOWS = 2


def spread_rows(key, shape):
    base = jnp.clip(jax.random.normal(jax.random.fold_in(key, 11), shape, jnp.float32), -6.0, 6.0)
    return base


def draw_query_latent(key, part):
    return spread_rows(key, (WINDOWS, TOKENS, QL)).astype(jnp.bfloat16)


def draw_kv_latent(key, part):
    return spread_rows(key, (WINDOWS, TOKENS, KVL + ROPE)).astype(jnp.bfloat16)


def draw_positions(key, part):
    token_index = jnp.arange(TOKENS, dtype=jnp.int32)
    first_end = 3 * TOKENS // 4
    marks = jax.random.randint(jax.random.fold_in(key, 21), (WINDOWS, TOKENS), 0, TOKENS) < 4
    marks = marks & (token_index[None, :] > first_end)
    marks = marks | (token_index[None, :] == 0) | (token_index[None, :] == first_end)
    starts = jnp.where(marks, token_index[None, :], 0).astype(jnp.int32)
    return (token_index[None, :] - lax.cummax(starts, axis=1)).astype(jnp.int32)


def shard_levels(rng, extent, split, least, largest):
    factor_of, own = 1.0, jax.random.fold_in(rng, 6)
    for dim, shards_of in split:
        draws = jnp.exp(jax.random.uniform(jax.random.fold_in(own, dim), (shards_of,), jnp.float32, least / len(split), largest / len(split)))
        factor_of = factor_of * jnp.repeat(draws, extent[dim] // shards_of).reshape([-1 if axis == dim else 1 for axis in range(len(extent))])
    return factor_of


def normal_values(key, shape, width, reach, shards=(), kind=jnp.bfloat16):
    values = width * jax.random.normal(key, shape, jnp.float32)
    if shards:
        values = values * shard_levels(key, shape, shards, -0.22, 0.18)
    return jnp.clip(values, -reach, reach).astype(kind)


def setup_inputs(seed: int = 0) -> dict:
    key_list = jax.random.split(jax.random.key(seed), 7)
    return {
        "query_latent": draw_query_latent(jax.random.fold_in(key_list[6], 71), 0),
        "kv_latent": draw_kv_latent(jax.random.fold_in(key_list[6], 71), 0),
        "query_up": normal_values(key_list[2], (QL, H * (NOPE + ROPE)), QL ** -0.5, 0.15625, ((1, 8),)),
        "kv_up": normal_values(key_list[3], (KVL, H * (NOPE + VD)), KVL ** -0.5, 0.25, ((1, 8),)),
        "out_grad": normal_values(key_list[4], (WINDOWS, TOKENS, H * VD), 1.0, 6.0, ((0, 2), (1, 16), (2, 8))),
        "positions": draw_positions(jax.random.fold_in(key_list[6], 71), 0),
    }


def rope_tables(positions):
    half_rope = ROPE // 2
    rotation_rates = 10000.0 ** (-jnp.arange(half_rope, dtype=jnp.float32) / half_rope)
    angles = positions.astype(jnp.float32)[:, None] * rotation_rates[None, :]
    return jnp.cos(angles), jnp.sin(angles)


def rotate(vector, cosine, sine_table):
    half_rope = ROPE // 2
    front_half = vector[..., :half_rope]
    back_half = vector[..., half_rope:]
    return jnp.concatenate([front_half * cosine - back_half * sine_table, front_half * sine_table + back_half * cosine], -1)


def unrotate(vector, cosine, sine_table):
    half_rope = ROPE // 2
    front_half = vector[..., :half_rope]
    back_half = vector[..., half_rope:]
    return jnp.concatenate([front_half * cosine + back_half * sine_table, back_half * cosine - front_half * sine_table], -1)


def window_grads(query_latent, kv_latent, query_up, kv_up, out_grad, positions):
    tokens = query_latent.shape[0]
    token_index = jnp.arange(tokens, dtype=jnp.int32)
    visible = (token_index[None, :] <= token_index[:, None]) & (
        (positions[:, None] - positions[None, :]) == (token_index[:, None] - token_index[None, :]))
    cosine, sine_table = rope_tables(positions)
    softmax_scale = (NOPE + ROPE) ** -0.5
    latent = kv_latent[:, :KVL]
    key_rope = kv_latent[:, KVL:].astype(jnp.float32)
    query_heads = query_up.reshape(QL, H, NOPE + ROPE).transpose(1, 0, 2)
    kv_heads = kv_up.reshape(KVL, H, NOPE + VD).transpose(1, 0, 2)
    grad_heads = out_grad.reshape(tokens, H, VD).transpose(1, 0, 2)

    def one_head(carry, operands):
        query_sum, latent_sum = carry
        query_weight, kv_weight, head_grad = operands
        projected_q = jnp.dot(query_latent, query_weight, preferred_element_type=jnp.float32)
        queries = jnp.concatenate([projected_q[:, :NOPE], rotate(projected_q[:, NOPE:], cosine, sine_table)], -1).astype(jnp.bfloat16)
        projected = jnp.dot(latent, kv_weight, preferred_element_type=jnp.float32)
        key_rows = jnp.concatenate([projected[:, :NOPE], key_rope], -1).astype(jnp.bfloat16)
        values = projected[:, NOPE:].astype(jnp.bfloat16)
        scores = jnp.dot(queries, key_rows.T, preferred_element_type=jnp.float32) * softmax_scale
        scores = jnp.where(visible, scores, -jnp.inf)
        row_max = jnp.max(scores, 1, keepdims=True)
        exponent = jnp.exp(scores - row_max)
        attention = exponent / jnp.sum(exponent, 1, keepdims=True)
        prob_grad = jnp.dot(head_grad, values.T, preferred_element_type=jnp.float32)
        row_inner = jnp.sum(attention * prob_grad, 1, keepdims=True)
        score_grad = (attention * (prob_grad - row_inner) * softmax_scale).astype(jnp.bfloat16)
        value_grad = jnp.dot(attention.astype(jnp.bfloat16).T, head_grad, preferred_element_type=jnp.float32).astype(jnp.bfloat16)
        query_rows_grad = jnp.dot(score_grad, key_rows, preferred_element_type=jnp.float32)
        key_grad = jnp.dot(score_grad.T, queries, preferred_element_type=jnp.float32).astype(jnp.bfloat16)
        head_query_grad = jnp.concatenate([query_rows_grad[:, :NOPE], unrotate(query_rows_grad[:, NOPE:], cosine, sine_table)], -1).astype(jnp.bfloat16)
        query_sum = query_sum + jnp.dot(head_query_grad, query_weight.T, preferred_element_type=jnp.float32)
        kv_rows_grad = jnp.concatenate([key_grad[:, :NOPE], value_grad], -1)
        latent_part = jnp.dot(kv_rows_grad, kv_weight.T, preferred_element_type=jnp.float32)
        latent_sum = latent_sum + jnp.concatenate([latent_part, key_grad[:, NOPE:].astype(jnp.float32)], -1)
        weight_grad = jnp.dot(query_latent.T, head_query_grad, preferred_element_type=jnp.float32)
        return (query_sum, latent_sum), weight_grad

    start_carry = (jnp.zeros((tokens, QL), jnp.float32), jnp.zeros((tokens, KVL + ROPE), jnp.float32))
    (query_sum, latent_sum), weight_grads = lax.scan(one_head, start_carry, (query_heads, kv_heads, grad_heads))
    return query_sum, latent_sum, weight_grads


def reference(query_latent, kv_latent, query_up, kv_up, out_grad, positions):
    query_list = []
    latent_list = []
    weight_total = jnp.zeros((H, QL, NOPE + ROPE), jnp.float32)
    for window in range(WINDOWS):
        query_sum, latent_sum, weight_grads = window_grads(query_latent[window], kv_latent[window], query_up, kv_up, out_grad[window], positions[window])
        query_list.append(query_sum)
        latent_list.append(latent_sum)
        weight_total = weight_total + weight_grads
    weight_out = weight_total.transpose(1, 0, 2).reshape(QL, H * (NOPE + ROPE)).astype(jnp.bfloat16)
    return (jnp.stack(query_list).astype(jnp.bfloat16), jnp.stack(latent_list).astype(jnp.bfloat16), weight_out)
```

```python
import jax
import jax.numpy as jnp
from jax import lax
from jax.experimental import pallas as pl
from jax.experimental.pallas import tpu as pltpu
from jax.sharding import PartitionSpec as P

QL = 1536
KVL = 512
ROPE = 64
NOPE = 128
VD = 128
HEADS = 8
TOK = 128
SLOTS = 12
SUB = 16
LAT = 640
KEYS = SLOTS * TOK
FIRST = 12
BF = jnp.bfloat16
F32 = jnp.float32
MESH = pl.DeviceIdType.MESH
VMEM_LIMIT = 63 * 1024 * 1024


def place():
    return lax.axis_index("rep"), lax.axis_index("seq"), lax.axis_index("head")


def group_base(s):
    return jnp.where(s < FIRST, 0, FIRST)


def z_partner(s):
    return s + 2 - 4 * lax.rem(lax.div(s, 2), 2)


def peer_rows(s):
    return lax.rem(lax.div(s, 2), 2)


def covered(z, zb, j):
    return lax.rem(jnp.where(zb == 0, z - j + 8, z + j), 8)


def remote(src, dst, send, recv, device):
    return pltpu.make_async_remote_copy(
        src_ref=src, dst_ref=dst, send_sem=send, recv_sem=recv, device_id=device, device_id_type=MESH
    )


def greet(devices_list):
    barrier = pltpu.get_barrier_semaphore()
    for device in devices_list:
        pl.semaphore_signal(barrier, inc=1, device_id=device, device_id_type=MESH)
    return barrier


def gather_kernel(kv_ref, xt_ref, lat_ref, xg_ref, s1, r1, s2, r2, sx, rx, lsem):
    r, s, h = place()
    base = group_base(s)
    slot = s - base
    z, zb = lax.div(s, 2), peer_rows(s)
    big = s < FIRST
    other = z_partner(s)
    quad = [(1 - r, s, h), (r, other, h), (1 - r, other, h)]
    plane = [(r, s, lax.rem(h + d, HEADS)) for d in range(1, HEADS)]

    barrier = greet(plane + quad)

    @pl.when(big)
    def _():
        for d in range(1, SLOTS):
            pl.semaphore_signal(
                barrier, inc=1, device_id=(r, lax.rem(slot + d, SLOTS), h), device_id_type=MESH
            )
        pl.semaphore_wait(barrier, SLOTS - 1 + 10)

    @pl.when(jnp.logical_not(big))
    def _():
        for d in range(1, 4):
            pl.semaphore_signal(
                barrier, inc=1, device_id=(r, FIRST + lax.rem(slot + d, 4), h), device_id_type=MESH
            )
        pl.semaphore_wait(barrier, 3 + 10)

    def to_seq(d, n):
        return remote(
            kv_ref.at[h], lat_ref.at[slot, h], s1.at[d], r1.at[d], (r, base + lax.rem(slot + d, n), h)
        )

    def from_seq(d, n):
        source = lax.rem(slot - d + n, n)
        return remote(kv_ref.at[h], lat_ref.at[source, h], s1.at[d], r1.at[d], (r, base + source, h))

    @pl.when(big)
    def _():
        for d in range(1, SLOTS):
            to_seq(d, SLOTS).start()

    @pl.when(jnp.logical_not(big))
    def _():
        for d in range(1, 4):
            to_seq(d, 4).start()
        for k in range(4, SLOTS):
            pltpu.make_async_copy(kv_ref.at[h], lat_ref.at[k, h], lsem.at[k]).start()

    pltpu.make_async_copy(kv_ref.at[h], lat_ref.at[slot, h], lsem.at[0]).start()

    mine = 2 * r + zb
    for k, (dr, dz) in enumerate(((1, 0), (0, 1), (1, 1))):
        pr = lax.rem(r + dr, 2)
        pzb = lax.rem(zb + dz, 2)
        ps = jnp.where(dz == 1, other, s)
        for j in range(4):
            zz = covered(lax.div(ps, 2), pzb, j)
            remote(
                xt_ref.at[pr, zz], xg_ref.at[mine, j], sx.at[k, j], rx.at[k, j], (pr, ps, h)
            ).start()
    for j in range(4):
        pltpu.make_async_copy(xt_ref.at[r, covered(z, zb, j)], xg_ref.at[mine, j], sx.at[3, j]).start()

    @pl.when(big)
    def _():
        for d in range(1, SLOTS):
            from_seq(d, SLOTS).wait_recv()

    @pl.when(jnp.logical_not(big))
    def _():
        for d in range(1, 4):
            from_seq(d, 4).wait_recv()
        for k in range(4, SLOTS):
            pltpu.make_async_copy(kv_ref.at[h], lat_ref.at[k, h], lsem.at[k]).wait()

    pltpu.make_async_copy(kv_ref.at[h], lat_ref.at[slot, h], lsem.at[0]).wait()

    for d in range(1, HEADS):
        remote(
            lat_ref.at[:, h], lat_ref.at[:, h], s2.at[d], r2.at[d], (r, s, lax.rem(h + d, HEADS))
        ).start()

    for k, (dr, dz) in enumerate(((1, 0), (0, 1), (1, 1))):
        source = 2 * lax.rem(r + dr, 2) + lax.rem(zb + dz, 2)
        for j in range(4):
            copy = remote(xt_ref.at[0, 0], xg_ref.at[source, j], sx.at[k, j], rx.at[k, j], (r, s, h))
            copy.wait_recv()
            copy.wait_send()
    for j in range(4):
        pltpu.make_async_copy(xt_ref.at[0, 0], xg_ref.at[mine, j], sx.at[3, j]).wait()
    for d in range(1, HEADS):
        source = lax.rem(h - d + HEADS, HEADS)
        copy = remote(lat_ref.at[:, h], lat_ref.at[:, source], s2.at[d], r2.at[d], (r, s, source))
        copy.wait_recv()
        copy.wait_send()

    @pl.when(big)
    def _():
        for d in range(1, SLOTS):
            to_seq(d, SLOTS).wait_send()

    @pl.when(jnp.logical_not(big))
    def _():
        for d in range(1, 4):
            to_seq(d, 4).wait_send()


def gather(kv, xt):
    dma = pltpu.SemaphoreType.DMA
    anyspace = pl.BlockSpec(memory_space=pl.ANY)
    return pl.pallas_call(
        gather_kernel,
        out_shape=(
            jax.ShapeDtypeStruct((SLOTS, HEADS, SUB, LAT), BF),
            jax.ShapeDtypeStruct((4, 4, 96, TOK), BF),
        ),
        in_specs=[anyspace] * 2,
        out_specs=(anyspace, anyspace),
        scratch_shapes=[
            dma((SLOTS,)), dma((SLOTS,)), dma((HEADS,)), dma((HEADS,)), dma((4, 4)), dma((4, 4)), dma((SLOTS,)),
        ],
        compiler_params=pltpu.CompilerParams(collective_id=0, has_side_effects=True),
        name="gather_latents",
    )(kv, xt)


NT = (((1,), (1,)), ((), ()))
TN = (((0,), (0,)), ((), ()))
NN = (((1,), (0,)), ((), ()))
PAIRS = HEADS // 2
ROWS = 128


def dot(a, b, dims):
    return lax.dot_general(a, b, dims, preferred_element_type=F32)


def swap_halves(v):
    lane = lax.broadcasted_iota(jnp.int32, v.shape, 1)
    half = ROPE // 2
    return jnp.where(lax.rem(lane, ROPE) < half, pltpu.roll(v, TOK - half, 1), pltpu.roll(v, half, 1))


def attention_kernel(
    x_ref, wq_ref, wkv_ref, do_ref, lat_ref, cos_ref, sin_ref, bounds_ref,
    dq_ref, dl_ref, qt_ref,
    a_s, r_s, kv_s, sp_s, sr_s, dp_s, dkv_s, rope_s,
):
    scale = (NOPE + ROPE) ** (-0.5)
    cosine, sine = cos_ref[...], sin_ref[...]
    left = lax.broadcasted_iota(jnp.int32, (TOK, TOK), 1) < ROPE
    projected = dot(x_ref[...], wq_ref[...], NN)
    for g in range(PAIRS):
        one, mid, last = (projected[:, 384 * g + TOK * k : 384 * g + TOK * (k + 1)] for k in range(3))
        two = jnp.where(left, pltpu.roll(mid, ROPE, 1), pltpu.roll(last, ROPE, 1))
        none = jnp.zeros((TOK, TOK), BF)
        for k, nope in enumerate((one, two)):
            i = 2 * g + k
            a_s[i, :TOK, :TOK] = nope.astype(BF)
            a_s[i, :TOK, TOK:] = none
            a_s[i, TOK:, :TOK] = none
            a_s[i, TOK:, TOK:] = do_ref[:, TOK * i : TOK * (i + 1)]
        r_s[g, :TOK, :] = jnp.where(left, mid * cosine + swap_halves(mid) * sine, 0.0).astype(BF)
        r_s[g, TOK:, :] = jnp.where(left, 0.0, last * cosine + swap_halves(last) * sine).astype(BF)
    rope_s[...] = jnp.zeros_like(rope_s)

    low = bounds_ref[0:1, :]
    high = bounds_ref[1:2, :]
    steps = KEYS // ROWS
    fold = (ROWS // 8, 8, TOK)
    both = range(2)

    def pair(g, carry):
        columns = pl.ds(pl.multiple_of(512 * g, 512), 512)
        kv_s[...] = dot(lat_ref[:, :KVL], wkv_ref[:, columns], NN).astype(BF)
        for k in both:
            sp_s[k] = dot(kv_s[:, 256 * k : 256 * (k + 1)], a_s[2 * g + k], NT)
        sr_s[...] = dot(lat_ref[:, KVL:], r_s[g], NT)

        def first(c, tops):
            at = pl.ds(pl.multiple_of(c * ROWS, ROWS), ROWS)
            key = c * ROWS + lax.broadcasted_iota(jnp.int32, (ROWS, TOK), 0)
            seen = (key >= low) & (key <= high)
            out = []
            for k in both:
                value = (sp_s[k, at, :TOK] + sr_s[at, TOK * k : TOK * (k + 1)]) * scale
                value = jnp.where(seen, value, -jnp.inf)
                sp_s[k, at, :TOK] = value
                out.append(jnp.maximum(tops[k], jnp.max(value.reshape(fold), 0)))
            return tuple(out)

        start = jnp.full((8, TOK), -jnp.inf, F32)
        tops = lax.fori_loop(0, steps, first, (start, start))
        tops = [jnp.max(top, 0, keepdims=True) for top in tops]

        def second(c, sums):
            at = pl.ds(pl.multiple_of(c * ROWS, ROWS), ROWS)
            out = []
            for k in both:
                value = jnp.exp(sp_s[k, at, :TOK] - tops[k])
                sp_s[k, at, :TOK] = value
                out.append(sums[2 * k] + jnp.sum(value.reshape(fold), 0))
                out.append(sums[2 * k + 1] + jnp.sum((value * sp_s[k, at, TOK:]).reshape(fold), 0))
            return tuple(out)

        zero = jnp.zeros((8, TOK), F32)
        sums = lax.fori_loop(0, steps, second, (zero,) * 4)
        inverse = [1.0 / jnp.sum(sums[2 * k], 0, keepdims=True) for k in both]
        inner = [jnp.sum(sums[2 * k + 1], 0, keepdims=True) * inverse[k] for k in both]

        def third(c, nothing):
            at = pl.ds(pl.multiple_of(c * ROWS, ROWS), ROWS)
            for k in both:
                weight = sp_s[k, at, :TOK] * inverse[k]
                dp_s[k, at, TOK:] = weight.astype(BF)
                dp_s[k, at, :TOK] = (weight * (sp_s[k, at, TOK:] - inner[k]) * scale).astype(BF)
            return nothing

        lax.fori_loop(0, steps, third, 0)
        nopes, ropes = [], []
        for k in both:
            score_grad = dp_s[k, :, :TOK]
            nopes.append(dot(score_grad, kv_s[:, 256 * k : 256 * k + NOPE], TN))
            chunk = dot(score_grad, lat_ref[:, KVL:], TN)
            ropes.append(chunk * cosine - swap_halves(chunk) * sine)
            dkv_s[g, :, 256 * k : 256 * (k + 1)] = dot(dp_s[k], a_s[2 * g + k], NN).astype(BF)
        second_nope = pltpu.roll(nopes[1], ROPE, 1)
        joined = jnp.concatenate(
            [nopes[0], jnp.where(left, ropes[0], second_nope), jnp.where(left, second_nope, ropes[1])], 1
        )
        dq_ref[:, pl.ds(pl.multiple_of(384 * g, 384), 384)] = joined.astype(BF)
        grads = jnp.concatenate([dp_s[0, :, :TOK], dp_s[1, :, :TOK]], 1)
        rope_s[...] += dot(grads, r_s[g], NN).astype(BF).astype(F32)
        return carry

    lax.fori_loop(0, PAIRS, pair, 0)
    qt_ref[...] = dot(dq_ref[...], wq_ref[...], NT).astype(BF)

    def latents(c, nothing):
        at = pl.ds(pl.multiple_of(c * 512, 512), 512)
        joined = jnp.concatenate([dkv_s[g, at, :] for g in range(PAIRS)], 1)
        dl_ref[at, :KVL] = dot(joined, wkv_ref[...], NT).astype(BF)
        rope = rope_s[at, :]
        dl_ref[at, KVL:] = (rope + pltpu.roll(rope, ROPE, 1)).astype(BF)
        return nothing

    lax.fori_loop(0, KEYS // 512, latents, 0)


def attention(x, wq, wkv, do, lat, cosine, sine, bounds):
    return pl.pallas_call(
        attention_kernel,
        out_shape=(
            jax.ShapeDtypeStruct((TOK, QL), BF),
            jax.ShapeDtypeStruct((KEYS, LAT), BF),
            jax.ShapeDtypeStruct((TOK, QL), BF),
        ),
        in_specs=[pl.BlockSpec(memory_space=pltpu.VMEM)] * 8,
        out_specs=(pl.BlockSpec(memory_space=pltpu.VMEM),) * 3,
        scratch_shapes=[
            pltpu.VMEM((HEADS, 2 * TOK, 2 * TOK), BF),
            pltpu.VMEM((PAIRS, 2 * TOK, TOK), BF),
            pltpu.VMEM((KEYS, 512), BF),
            pltpu.VMEM((2, KEYS, 2 * TOK), F32),
            pltpu.VMEM((KEYS, 2 * TOK), F32),
            pltpu.VMEM((2, KEYS, 2 * TOK), BF),
            pltpu.VMEM((PAIRS, KEYS, 512), BF),
            pltpu.VMEM((KEYS, TOK), F32),
        ],
        compiler_params=pltpu.CompilerParams(vmem_limit_bytes=VMEM_LIMIT),
        name="attention_backward",
    )(x, wq, wkv, do, lat, cosine, sine, bounds)


def exchange_kernel(dq_ref, dl_ref, qt_ref, dg_ref, rl_ref, rq_ref, ss, rs, sq, rq, sd, rd, lsem):
    r, s, h = place()
    zb = peer_rows(s)
    other = z_partner(s)
    quad = [(1 - r, s, h), (r, other, h), (1 - r, other, h)]
    plane = [(r, s, lax.rem(h + d, HEADS)) for d in range(1, HEADS)]
    barrier = greet(plane + quad)
    pl.semaphore_wait(barrier, 10)
    mine = 2 * r + zb
    for k, device in enumerate(quad):
        remote(dq_ref, dg_ref.at[mine], sd.at[k], rd.at[k], device).start()
    for d in range(1, HEADS):
        peer = lax.rem(h + d, HEADS)
        remote(dl_ref.at[:, peer], rl_ref.at[h], ss.at[d], rs.at[d], (r, s, peer)).start()
        remote(qt_ref.at[peer], rq_ref.at[h], sq.at[d], rq.at[d], (r, s, peer)).start()
    local = [
        pltpu.make_async_copy(dq_ref, dg_ref.at[mine], lsem.at[0]),
        pltpu.make_async_copy(dl_ref.at[:, h], rl_ref.at[h], lsem.at[1]),
        pltpu.make_async_copy(qt_ref.at[h], rq_ref.at[h], lsem.at[2]),
    ]
    for copy in local:
        copy.start()
    for copy in local:
        copy.wait()
    for k, (dr, dz) in enumerate(((1, 0), (0, 1), (1, 1))):
        source = 2 * lax.rem(r + dr, 2) + lax.rem(zb + dz, 2)
        copy = remote(dq_ref, dg_ref.at[source], sd.at[k], rd.at[k], quad[k])
        copy.wait_recv()
        copy.wait_send()
    for d in range(1, HEADS):
        source = lax.rem(h - d + HEADS, HEADS)
        copy = remote(dl_ref.at[:, h], rl_ref.at[source], ss.at[d], rs.at[d], (r, s, source))
        copy.wait_recv()
        copy.wait_send()
        copy = remote(qt_ref.at[h], rq_ref.at[source], sq.at[d], rq.at[d], (r, s, source))
        copy.wait_recv()
        copy.wait_send()


def exchange(dq, dl, qt):
    dma = pltpu.SemaphoreType.DMA
    anyspace = pl.BlockSpec(memory_space=pl.ANY)
    return pl.pallas_call(
        exchange_kernel,
        out_shape=(
            jax.ShapeDtypeStruct((4, TOK, QL), BF),
            jax.ShapeDtypeStruct((HEADS, SLOTS, SUB, LAT), BF),
            jax.ShapeDtypeStruct((HEADS, SUB, QL), BF),
        ),
        in_specs=[anyspace] * 3,
        out_specs=(anyspace,) * 3,
        scratch_shapes=[dma((HEADS,)), dma((HEADS,)), dma((HEADS,)), dma((HEADS,)), dma((3,)), dma((3,)), dma((3,))],
        compiler_params=pltpu.CompilerParams(collective_id=1, has_side_effects=True),
        name="exchange_terms",
    )(dq, dl, qt)


def combine_kernel(xg_ref, dg_ref, rl_ref, rq_ref, w_ref, ls_ref, qs_ref):
    left = jnp.concatenate([xg_ref[k].reshape(4 * 96, TOK) for k in range(4)], 1)
    right = dg_ref[...].reshape(4 * TOK, QL)
    w_ref[...] = dot(left, right, NN).astype(BF)
    total = rq_ref[0].astype(F32)
    for k in range(1, HEADS):
        total += rq_ref[k].astype(F32)
    qs_ref[...] = total.astype(BF)
    for c in range(SLOTS):
        total = rl_ref[0, c].astype(F32)
        for k in range(1, HEADS):
            total += rl_ref[k, c].astype(F32)
        ls_ref[c] = total.astype(BF)


def combine(xg, dg, rl, rq):
    return pl.pallas_call(
        combine_kernel,
        out_shape=(
            jax.ShapeDtypeStruct((4 * 96, QL), BF),
            jax.ShapeDtypeStruct((SLOTS, SUB, LAT), BF),
            jax.ShapeDtypeStruct((SUB, QL), BF),
        ),
        in_specs=[pl.BlockSpec(memory_space=pltpu.VMEM)] * 4,
        out_specs=(pl.BlockSpec(memory_space=pltpu.VMEM),) * 3,
        compiler_params=pltpu.CompilerParams(vmem_limit_bytes=VMEM_LIMIT),
        name="combine_terms",
    )(xg, dg, rl, rq)


def source_z(z, j):
    down = lax.rem(z + j, 8)
    up = lax.rem(z - j + 8, 8)
    return jnp.where(lax.rem(down, 2) == 0, down, up)


def deliver_kernel(w_ref, ls_ref, qs_ref, rw_ref, rl_ref, qg_ref, sw, rw, sl, rl, sq, rq, lsem):
    r, s, h = place()
    base = group_base(s)
    slot = s - base
    big = s < FIRST
    z, zb, yh = lax.div(s, 2), peer_rows(s), lax.rem(s, 2)
    plane = [(r, s, lax.rem(h + d, HEADS)) for d in range(1, HEADS)]
    steps = [(j, y) for j in range(4) for y in range(2)][1:]
    owners = [(j, y, (r, 2 * covered(z, zb, j) + lax.rem(yh + y, 2), h)) for j, y in steps]
    sources = [(j, y, (r, 2 * source_z(z, j) + lax.rem(yh + y, 2), h)) for j, y in steps]
    barrier = greet(plane + [device for _, _, device in sources])

    @pl.when(big)
    def _():
        for d in range(1, SLOTS):
            pl.semaphore_signal(
                barrier, inc=1, device_id=(r, lax.rem(slot + d, SLOTS), h), device_id_type=MESH
            )
        pl.semaphore_wait(barrier, SLOTS - 1 + 14)

    @pl.when(jnp.logical_not(big))
    def _():
        for d in range(1, 4):
            pl.semaphore_signal(
                barrier, inc=1, device_id=(r, FIRST + lax.rem(slot + d, 4), h), device_id_type=MESH
            )
        pl.semaphore_wait(barrier, 3 + 14)

    for j, y, device in owners:
        remote(w_ref.at[j, lax.rem(yh + y, 2)], rw_ref.at[j, y], sw.at[j, y], rw.at[j, y], device).start()

    def send_latent(d, n):
        peer = lax.rem(slot + d, n)
        return remote(ls_ref.at[peer], rl_ref.at[slot], sl.at[d], rl.at[d], (r, base + peer, h))

    def take_latent(d, n):
        peer = lax.rem(slot - d + n, n)
        return remote(ls_ref.at[0], rl_ref.at[peer], sl.at[d], rl.at[d], (r, base + peer, h))

    @pl.when(big)
    def _():
        for d in range(1, SLOTS):
            send_latent(d, SLOTS).start()

    @pl.when(jnp.logical_not(big))
    def _():
        for d in range(1, 4):
            send_latent(d, 4).start()

    for d in range(1, HEADS):
        remote(qs_ref, qg_ref.at[h], sq.at[d], rq.at[d], (r, s, lax.rem(h + d, HEADS))).start()
    local = [
        pltpu.make_async_copy(w_ref.at[0, yh], rw_ref.at[0, 0], lsem.at[0]),
        pltpu.make_async_copy(ls_ref.at[slot], rl_ref.at[slot], lsem.at[1]),
        pltpu.make_async_copy(qs_ref, qg_ref.at[h], lsem.at[2]),
    ]
    for copy in local:
        copy.start()
    for copy in local:
        copy.wait()

    for d in range(1, HEADS):
        source = lax.rem(h - d + HEADS, HEADS)
        copy = remote(qs_ref, qg_ref.at[source], sq.at[d], rq.at[d], (r, s, source))
        copy.wait_recv()
        copy.wait_send()

    @pl.when(big)
    def _():
        for d in range(1, SLOTS):
            take_latent(d, SLOTS).wait_recv()
            send_latent(d, SLOTS).wait_send()

    @pl.when(jnp.logical_not(big))
    def _():
        for d in range(1, 4):
            take_latent(d, 4).wait_recv()
            send_latent(d, 4).wait_send()

    for j, y, device in sources:
        copy = remote(w_ref.at[j, 0], rw_ref.at[j, y], sw.at[j, y], rw.at[j, y], device)
        copy.wait_recv()
        copy.wait_send()


def deliver(w, ls, qs):
    dma = pltpu.SemaphoreType.DMA
    anyspace = pl.BlockSpec(memory_space=pl.ANY)
    return pl.pallas_call(
        deliver_kernel,
        out_shape=(
            jax.ShapeDtypeStruct((4, 2, 48, QL), BF),
            jax.ShapeDtypeStruct((SLOTS, SUB, LAT), BF),
            jax.ShapeDtypeStruct((HEADS, SUB, QL), BF),
        ),
        in_specs=[anyspace] * 3,
        out_specs=(anyspace,) * 3,
        scratch_shapes=[
            dma((4, 2)), dma((4, 2)), dma((SLOTS,)), dma((SLOTS,)), dma((HEADS,)), dma((HEADS,)), dma((3,)),
        ],
        compiler_params=pltpu.CompilerParams(collective_id=2, has_side_effects=True),
        name="deliver_sums",
    )(w, ls, qs)


def finish_kernel(rw_ref, rl_ref, count_ref, w_ref, l_ref):
    total = rw_ref[0, 0].astype(F32)
    for k in range(1, 8):
        total += rw_ref[k // 2, k % 2].astype(F32)
    w_ref[...] = total.astype(BF)
    count = count_ref[0]
    total = jnp.zeros((SUB, LAT), F32)
    for k in range(SLOTS):
        total += jnp.where(k < count, rl_ref[k].astype(F32), 0.0)
    l_ref[...] = total[:, : KVL + ROPE].astype(BF)


def finish(rw, rl, count):
    return pl.pallas_call(
        finish_kernel,
        out_shape=(
            jax.ShapeDtypeStruct((48, QL), BF),
            jax.ShapeDtypeStruct((SUB, KVL + ROPE), BF),
        ),
        in_specs=[pl.BlockSpec(memory_space=pltpu.VMEM)] * 2 + [pl.BlockSpec(memory_space=pltpu.SMEM)],
        out_specs=(pl.BlockSpec(memory_space=pltpu.VMEM),) * 2,
        name="finish_sums",
    )(rw, rl, count)


def shards(query_latent, kv_latent, query_up, kv_up, out_grad, positions):
    s = lax.axis_index("seq")
    x = query_latent[0]
    first_row = s * TOK
    local_positions = lax.dynamic_slice_in_dim(positions[0], first_row, TOK)
    index = first_row + jnp.arange(TOK, dtype=jnp.int32) - group_base(s) * TOK
    bounds = jnp.stack([index - local_positions, index] + [index] * 6)
    half = ROPE // 2
    rates = 10000.0 ** (-jnp.arange(half, dtype=F32) / half)
    angles = local_positions.astype(F32)[:, None] * rates[None, :]
    cosine, sine = jnp.cos(angles), jnp.sin(angles)
    cosine_table = jnp.concatenate([cosine] * 4, 1)
    sine_table = jnp.concatenate([-sine, sine] * 2, 1)
    kv = jnp.concatenate([kv_latent[0], kv_latent[0][:, KVL:]], 1).reshape(HEADS, SUB, LAT)
    xt = x.T.reshape(2, 8, 96, TOK)

    lat, xg = gather(kv, xt)
    dq, dl, qt = attention(
        x, query_up, kv_up, out_grad[0], lat.reshape(KEYS, LAT), cosine_table, sine_table, bounds
    )
    dg, rl, rq = exchange(dq, dl.reshape(SLOTS, HEADS, SUB, LAT), qt.reshape(HEADS, SUB, QL))
    w, ls, qs = combine(xg, dg, rl, rq)
    rw, rlat, qg = deliver(w.reshape(4, 2, 48, QL), ls, qs)
    count = jnp.where(s < FIRST, SLOTS, 4).astype(jnp.int32).reshape(1)
    weight_grad, latent_grad = finish(rw, rlat, count)
    return qg.reshape(1, TOK, QL), latent_grad[None], weight_grad


def solution(mesh):
    return jax.shard_map(
        shards,
        mesh=mesh,
        in_specs=(
            P("rep", "seq", None),
            P("rep", "seq", None),
            P(None, "head"),
            P(None, "head"),
            P("rep", "seq", "head"),
            P("rep", None),
        ),
        out_specs=(
            P("rep", "seq", None),
            P("rep", ("seq", "head"), None),
            P(("rep", "seq"), "head"),
        ),
        check_vma=False,
    )
```

```python
import jax
import jax.numpy as jnp
from jax import lax
from jax.experimental import pallas as pl
from jax.experimental.pallas import tpu as pltpu
from jax.sharding import PartitionSpec as P

QL = 1536
KVL = 512
ROPE = 64
NOPE = 128
VD = 128
HEADS = 8
TOK = 128
SLOTS = 12
SUB = 16
LAT = 640
KEYS = SLOTS * TOK
FIRST = 12
BF = jnp.bfloat16
F32 = jnp.float32
MESH = pl.DeviceIdType.MESH
VMEM_LIMIT = 63 * 1024 * 1024


def place():
    return lax.axis_index("rep"), lax.axis_index("seq"), lax.axis_index("head")


def group_base(s):
    return jnp.where(s < FIRST, 0, FIRST)


def z_partner(s):
    return s + 2 - 4 * lax.rem(lax.div(s, 2), 2)


def peer_rows(s):
    return lax.rem(lax.div(s, 2), 2)


def covered(z, zb, j):
    return lax.rem(jnp.where(zb == 0, z - j + 8, z + j), 8)


def remote(src, dst, send, recv, device):
    return pltpu.make_async_remote_copy(
        src_ref=src, dst_ref=dst, send_sem=send, recv_sem=recv, device_id=device, device_id_type=MESH
    )


def source_z(z, j):
    down = lax.rem(z + j, 8)
    up = lax.rem(z - j + 8, 8)
    return jnp.where(lax.rem(down, 2) == 0, down, up)


NT = (((1,), (1,)), ((), ()))
TN = (((0,), (0,)), ((), ()))
NN = (((1,), (0,)), ((), ()))
PAIRS = HEADS // 2
PARTS = 3
CHUNK = KEYS // PARTS
ROWS = 128


def dot(a, b, dims):
    return lax.dot_general(a, b, dims, preferred_element_type=F32)


def swap_halves(v):
    lane = lax.broadcasted_iota(jnp.int32, v.shape, 1)
    half = ROPE // 2
    return jnp.where(lax.rem(lane, ROPE) < half, pltpu.roll(v, TOK - half, 1), pltpu.roll(v, half, 1))


PIECES = [(j, y) for j in range(4) for y in range(2)]
TURNS = ((1, 0), (0, 1), (1, 1))


def kernel(
    x_ref, kv_ref, wq_hbm, wkv_hbm, do_ref, trig_ref, pos_ref,
    qg_ref, w_ref, l_ref,
    wq_v, wkv_v, kvx_s, xt_s, lat_s, xg_s, a_s, r_s, kvd_s, sp_s, sr_s, dp_s, rope_s, acc_s,
    dg_s, wp_s, rw_s, qt_s, rq_s, qs_s, dl_s, rl_s, ls_s, rlat_s,
    load, s1, r1, s2, r2, sx, rx, sdq, rdq, sw, rw, sqt, rqt, sqa, rqa, sdl, rdl, sls, rls,
):
    r, s, h = place()
    big = s < FIRST
    base = group_base(s)
    slot = s - base
    members = jnp.where(big, SLOTS, 4)
    part = lax.div(slot, 4)
    parts = part + 1
    z, zb, yh = lax.div(s, 2), peer_rows(s), lax.rem(s, 2)
    other = z_partner(s)
    mine = 2 * r + zb
    sibling, partner, diagonal = (1 - r, s, h), (r, other, h), (1 - r, other, h)
    plane = [lax.rem(h + d, HEADS) for d in range(1, HEADS)]
    owners = [(r, 2 * covered(z, zb, j) + lax.rem(yh + y, 2), h) for j, y in PIECES]
    sources = [(r, 2 * source_z(z, j) + lax.rem(yh + y, 2), h) for j, y in PIECES]

    barrier = pltpu.get_barrier_semaphore()

    def signal(device):
        pl.semaphore_signal(barrier, inc=1, device_id=device, device_id_type=MESH)

    for peer in plane:
        signal((r, s, peer))
    for device in (sibling, partner, diagonal):
        signal(device)
    for device in sources[1:]:
        signal(device)
    for k in range(SLOTS):
        @pl.when((k != slot) & (k < members))
        def _():
            signal((r, base + k, h))

    loads = [
        pltpu.make_async_copy(wq_hbm, wq_v, load.at[0]),
        pltpu.make_async_copy(wkv_hbm, wkv_v, load.at[1]),
    ]
    for copy in loads:
        copy.start()
    kvx_s[...] = jnp.concatenate([kv_ref[...], kv_ref[:, KVL:]], 1).reshape(HEADS, SUB, LAT)
    xt_s[...] = x_ref[...].T.reshape(2, 8, 96, TOK)
    lat_s[slot, h] = kvx_s[h]
    pl.semaphore_wait(barrier, members - 1 + 17)

    def to_seq(k):
        return remote(kvx_s.at[h], lat_s.at[slot, h], s1.at[k], r1.at[slot], (r, base + k, h))

    def from_seq(k):
        return remote(kvx_s.at[h], lat_s.at[k, h], s1.at[k], r1.at[k], (r, base + k, h))

    def fresh(k):
        return (k != slot) & (k < members) & (k // 4 >= part)

    def older(k):
        return (k != slot) & (k < members) & (k // 4 <= part)

    for k in range(SLOTS):
        @pl.when(fresh(k))
        def _():
            to_seq(k).start()

    def columns(k, dr, dz, j):
        pr, pzb = lax.rem(r + dr, 2), lax.rem(zb + dz, 2)
        ps = other if dz else s
        return remote(
            xt_s.at[pr, covered(lax.div(ps, 2), pzb, j)], xg_s.at[mine, j], sx.at[k, j], rx.at[k, j], (pr, ps, h)
        )

    for k, (dr, dz) in enumerate(TURNS):
        for j in range(4):
            columns(k, dr, dz, j).start()
    for j in range(4):
        xg_s[mine, j] = xt_s[r, covered(z, zb, j)]

    def slots_of(p):
        return pl.ds(pl.multiple_of(4 * p, 4), 4)

    def to_plane(p, d):
        return remote(
            lat_s.at[slots_of(p), h], lat_s.at[slots_of(p), h], s2.at[p, d], r2.at[p, d], (r, s, plane[d - 1])
        )

    def from_plane(p, d):
        source = lax.rem(h - d + HEADS, HEADS)
        return remote(
            lat_s.at[slots_of(p), h], lat_s.at[slots_of(p), source], s2.at[p, d], r2.at[p, d], (r, s, source)
        )

    for p in range(PARTS):
        for k in range(4 * p, 4 * p + 4):
            @pl.when(older(k))
            def _():
                from_seq(k).wait_recv()

        @pl.when(p < parts)
        def _():
            for d in range(1, HEADS):
                to_plane(p, d).start()

    scale = (NOPE + ROPE) ** (-0.5)
    cosine = jnp.concatenate([trig_ref[:, : ROPE // 2]] * 4, 1)
    sine = jnp.concatenate([-trig_ref[:, ROPE // 2 :], trig_ref[:, ROPE // 2 :]] * 2, 1)
    left = lax.broadcasted_iota(jnp.int32, (TOK, TOK), 1) < ROPE
    loads[0].wait()
    for g in range(PAIRS):
        projected = dot(x_ref[...], wq_v[:, 384 * g : 384 * (g + 1)], NN)
        one, mid, last = (projected[:, TOK * k : TOK * (k + 1)] for k in range(3))
        two = jnp.where(left, pltpu.roll(mid, ROPE, 1), pltpu.roll(last, ROPE, 1))
        none = jnp.zeros((TOK, TOK), BF)
        for k, nope in enumerate((one, two)):
            i = 2 * g + k
            a_s[i, :TOK, :TOK] = nope.astype(BF)
            a_s[i, :TOK, TOK:] = none
            a_s[i, TOK:, :TOK] = none
            a_s[i, TOK:, TOK:] = do_ref[:, TOK * i : TOK * (i + 1)]
        r_s[g, :TOK, :] = jnp.where(left, mid * cosine + swap_halves(mid) * sine, 0.0).astype(BF)
        r_s[g, TOK:, :] = jnp.where(left, 0.0, last * cosine + swap_halves(last) * sine).astype(BF)
    rope_s[...] = jnp.zeros_like(rope_s)
    loads[1].wait()

    def chunk_at(p):
        return pl.ds(pl.multiple_of(p * CHUNK, CHUNK), CHUNK)

    def latent_chunk(p):
        return lat_s[slots_of(p)].reshape(CHUNK, LAT)

    def keys_of(p, nothing):
        for d in range(1, HEADS):
            from_plane(p, d).wait_recv()
        rows = latent_chunk(p)[:, :KVL]
        for g in range(PAIRS):
            kvd_s[g, chunk_at(p), :] = dot(rows, wkv_v[:, 512 * g : 512 * (g + 1)], NN).astype(BF)
        return nothing

    lax.fori_loop(0, parts, keys_of, 0)
    for k, (dr, dz) in enumerate(TURNS):
        source = 2 * lax.rem(r + dr, 2) + lax.rem(zb + dz, 2)
        for j in range(4):
            remote(xt_s.at[0, 0], xg_s.at[source, j], sx.at[k, j], rx.at[k, j], sibling).wait_recv()

    first_row = pl.ds(pl.multiple_of(s * TOK, TOK), TOK)
    high = slot * TOK + lax.broadcasted_iota(jnp.int32, (1, TOK), 1)
    low = high - pos_ref[:, first_row]
    steps = parts * (CHUNK // ROWS)
    fold = (ROWS // 8, 8, TOK)
    both = range(2)

    def hand_out(g, k):
        source = mine if k < 2 else 2 * r + 1 - zb
        return remote(dg_s.at[g, source], dg_s.at[g, source], sdq.at[g, k], rdq.at[g, k], partner if k == 1 else sibling)

    def hand_in(g, k):
        source = (2 * (1 - r) + zb, 2 * r + 1 - zb, 2 * (1 - r) + 1 - zb)[k]
        return remote(dg_s.at[g, source], dg_s.at[g, source], sdq.at[g, k], rdq.at[g, k], sibling)

    def relay(g):
        hand_in(g, 1).wait_recv()
        hand_out(g, 2).start()

    def to_owner(g, n):
        j, y = PIECES[n]
        return remote(
            wp_s.at[g, j, lax.rem(yh + y, 2)], rw_s.at[g, j, y], sw.at[g, n], rw.at[g, n], owners[n]
        )

    def from_source(g, n):
        j, y = PIECES[n]
        return remote(wp_s.at[g, j, y], rw_s.at[g, j, y], sw.at[g, n], rw.at[g, n], sources[n])

    def weights(g):
        hand_in(g, 0).wait_recv()
        hand_in(g, 2).wait_recv()
        rows = jnp.concatenate([xg_s[k].reshape(4 * 96, TOK) for k in range(4)], 1)
        product = dot(rows, dg_s[g].reshape(4 * TOK, 384), NN)
        wp_s[g] = product.astype(BF).reshape(4, 2, 48, 384)
        for n in range(1, 8):
            to_owner(g, n).start()

    def pair(g, carry):
        def scores(p, nothing):
            at = chunk_at(p)
            for k in both:
                sp_s[k, at, :] = dot(kvd_s[g, at, 256 * k : 256 * (k + 1)], a_s[2 * g + k], NT)
            sr_s[at, :] = dot(latent_chunk(p)[:, KVL:], r_s[g], NT)
            return nothing

        lax.fori_loop(0, parts, scores, 0)

        def first(c, tops):
            at = pl.ds(pl.multiple_of(c * ROWS, ROWS), ROWS)
            key = c * ROWS + lax.broadcasted_iota(jnp.int32, (ROWS, TOK), 0)
            seen = (key >= low) & (key <= high)
            out = []
            for k in both:
                value = (sp_s[k, at, :TOK] + sr_s[at, TOK * k : TOK * (k + 1)]) * scale
                value = jnp.where(seen, value, -jnp.inf)
                sp_s[k, at, :TOK] = value
                out.append(jnp.maximum(tops[k], jnp.max(value.reshape(fold), 0)))
            return tuple(out)

        start = jnp.full((8, TOK), -jnp.inf, F32)
        tops = lax.fori_loop(0, steps, first, (start, start))
        tops = [jnp.max(top, 0, keepdims=True) for top in tops]

        def second(c, sums):
            at = pl.ds(pl.multiple_of(c * ROWS, ROWS), ROWS)
            out = []
            for k in both:
                value = jnp.exp(sp_s[k, at, :TOK] - tops[k])
                sp_s[k, at, :TOK] = value
                out.append(sums[2 * k] + jnp.sum(value.reshape(fold), 0))
                out.append(sums[2 * k + 1] + jnp.sum((value * sp_s[k, at, TOK:]).reshape(fold), 0))
            return tuple(out)

        zero = jnp.zeros((8, TOK), F32)
        sums = lax.fori_loop(0, steps, second, (zero,) * 4)
        inverse = [1.0 / jnp.sum(sums[2 * k], 0, keepdims=True) for k in both]
        inner = [jnp.sum(sums[2 * k + 1], 0, keepdims=True) * inverse[k] for k in both]

        @pl.when(g >= 1)
        def _():
            relay(g - 1)

        def third(c, nothing):
            at = pl.ds(pl.multiple_of(c * ROWS, ROWS), ROWS)
            for k in both:
                weight = sp_s[k, at, :TOK] * inverse[k]
                dp_s[k, at, TOK:] = weight.astype(BF)
                dp_s[k, at, :TOK] = (weight * (sp_s[k, at, TOK:] - inner[k]) * scale).astype(BF)
            return nothing

        lax.fori_loop(0, steps, third, 0)
        acc_s[...] = jnp.zeros_like(acc_s)

        def backward(p, nothing):
            at = chunk_at(p)
            key_rope = latent_chunk(p)[:, KVL:]
            for k in both:
                score_grad = dp_s[k, at, :TOK]
                rows = jnp.concatenate([kvd_s[g, at, 256 * k : 256 * k + NOPE], key_rope], 1)
                acc_s[k] += dot(score_grad, rows, TN)
                kvd_s[g, at, 256 * k : 256 * (k + 1)] = dot(dp_s[k, at, :], a_s[2 * g + k], NN).astype(BF)
            grads = jnp.concatenate([dp_s[0, at, :TOK], dp_s[1, at, :TOK]], 1)
            rope_s[at, :] += dot(grads, r_s[g], NN).astype(BF).astype(F32)
            return nothing

        lax.fori_loop(0, parts, backward, 0)
        ropes = []
        for k in both:
            chunk = acc_s[k, :, TOK:]
            ropes.append(chunk * cosine - swap_halves(chunk) * sine)
        second_nope = pltpu.roll(acc_s[1, :, :TOK], ROPE, 1)
        dg_s[g, mine] = jnp.concatenate(
            [acc_s[0, :, :TOK], jnp.where(left, ropes[0], second_nope), jnp.where(left, second_nope, ropes[1])], 1
        ).astype(BF)
        hand_out(g, 0).start()
        hand_out(g, 1).start()

        @pl.when(g >= 1)
        def _():
            weights(g - 1)

        return carry

    lax.fori_loop(0, PAIRS, pair, 0)

    joined = jnp.concatenate([dg_s[g, mine] for g in range(PAIRS)], 1)
    qt_s[...] = dot(joined, wq_v[...], NT).astype(BF).reshape(HEADS, SUB, QL)

    def query_out(d):
        return remote(qt_s.at[plane[d - 1]], rq_s.at[h], sqt.at[d], rqt.at[d], (r, s, plane[d - 1]))

    for d in range(1, HEADS):
        query_out(d).start()
    relay(PAIRS - 1)

    def latent_out(p, d):
        return remote(
            dl_s.at[slots_of(p), plane[d - 1]], rl_s.at[h, slots_of(p)], sdl.at[p, d], rdl.at[p, d],
            (r, s, plane[d - 1]),
        )

    def latent_in(p, d):
        source = lax.rem(h - d + HEADS, HEADS)
        return remote(
            dl_s.at[slots_of(p), h], rl_s.at[source, slots_of(p)], sdl.at[p, d], rdl.at[p, d], (r, s, source)
        )

    def latents(p, nothing):
        at = chunk_at(p)
        rows = jnp.concatenate([kvd_s[g, at, :] for g in range(PAIRS)], 1)
        low_part = dot(rows, wkv_v[...], NT).astype(BF)
        rope = rope_s[at, :]
        rope = (rope + pltpu.roll(rope, ROPE, 1)).astype(BF)
        dl_s[slots_of(p)] = jnp.concatenate([low_part, rope], 1).reshape(4, HEADS, SUB, LAT)
        for d in range(1, HEADS):
            latent_out(p, d).start()
        return nothing

    lax.fori_loop(0, parts, latents, 0)
    weights(PAIRS - 1)

    total = qt_s[h].astype(F32)
    for d in range(1, HEADS):
        source = lax.rem(h - d + HEADS, HEADS)
        remote(qt_s.at[h], rq_s.at[source], sqt.at[d], rqt.at[d], (r, s, source)).wait_recv()
        total += rq_s[source].astype(F32)
    qs_s[...] = total.astype(BF)
    qg_ref[h] = qs_s[...]

    def query_share(d):
        return remote(qs_s, qg_ref.at[h], sqa.at[d], rqa.at[d], (r, s, plane[d - 1]))

    for d in range(1, HEADS):
        query_share(d).start()

    def to_latent_owner(k):
        return remote(ls_s.at[k], rlat_s.at[slot], sls.at[k], rls.at[slot], (r, base + k, h))

    def from_latent_source(k):
        return remote(ls_s.at[k], rlat_s.at[k], sls.at[k], rls.at[k], (r, base + k, h))

    for p in range(PARTS):
        @pl.when(p < parts)
        def _():
            for d in range(1, HEADS):
                latent_in(p, d).wait_recv()
            for k in range(4 * p, 4 * p + 4):
                total = dl_s[k, h].astype(F32)
                for d in range(1, HEADS):
                    total += rl_s[lax.rem(h + d, HEADS), k].astype(F32)
                ls_s[k] = total.astype(BF)

                @pl.when(older(k))
                def _():
                    to_latent_owner(k).start()

    for g in range(PAIRS):
        total = wp_s[g, 0, yh].astype(F32)
        for n in range(1, 8):
            from_source(g, n).wait_recv()
            total += rw_s[g, n // 2, n % 2].astype(F32)
        w_ref[:, 384 * g : 384 * (g + 1)] = total.astype(BF)

    acc_s[0, :SUB, :] = ls_s[slot, :, :256].astype(F32)
    acc_s[0, SUB : 2 * SUB, :] = ls_s[slot, :, 256:512].astype(F32)
    acc_s[0, 2 * SUB : 3 * SUB, :TOK] = ls_s[slot, :, 512:].astype(F32)
    for k in range(SLOTS):
        @pl.when(fresh(k))
        def _():
            from_latent_source(k).wait_recv()
            acc_s[0, :SUB, :] += rlat_s[k, :, :256].astype(F32)
            acc_s[0, SUB : 2 * SUB, :] += rlat_s[k, :, 256:512].astype(F32)
            acc_s[0, 2 * SUB : 3 * SUB, :TOK] += rlat_s[k, :, 512:].astype(F32)
    l_ref[...] = jnp.concatenate(
        [acc_s[0, :SUB, :], acc_s[0, SUB : 2 * SUB, :], acc_s[0, 2 * SUB : 3 * SUB, :ROPE]], 1
    ).astype(BF)

    for d in range(1, HEADS):
        source = lax.rem(h - d + HEADS, HEADS)
        remote(qs_s, qg_ref.at[source], sqa.at[d], rqa.at[d], (r, s, source)).wait_recv()
        query_share(d).wait_send()
        query_out(d).wait_send()
    for k in range(SLOTS):
        @pl.when(fresh(k))
        def _():
            to_seq(k).wait_send()

        @pl.when(older(k))
        def _():
            to_latent_owner(k).wait_send()
    for k, (dr, dz) in enumerate(TURNS):
        for j in range(4):
            columns(k, dr, dz, j).wait_send()

    def drain_part(p, nothing):
        for d in range(1, HEADS):
            to_plane(p, d).wait_send()
            latent_out(p, d).wait_send()
        return nothing

    lax.fori_loop(0, parts, drain_part, 0)

    def drain_pair(g, nothing):
        for k in range(3):
            hand_out(g, k).wait_send()
        for n in range(1, 8):
            to_owner(g, n).wait_send()
        return nothing

    lax.fori_loop(0, PAIRS, drain_pair, 0)


def backward_pass(x, kv, wq, wkv, do, trig, positions):
    dma = pltpu.SemaphoreType.DMA
    vmem = pl.BlockSpec(memory_space=pltpu.VMEM)
    hbm = pl.BlockSpec(memory_space=pl.ANY)
    return pl.pallas_call(
        kernel,
        out_shape=(
            jax.ShapeDtypeStruct((HEADS, SUB, QL), BF),
            jax.ShapeDtypeStruct((48, QL), BF),
            jax.ShapeDtypeStruct((SUB, KVL + ROPE), BF),
        ),
        in_specs=[vmem, vmem, hbm, hbm, vmem, vmem, vmem],
        out_specs=(vmem,) * 3,
        scratch_shapes=[
            pltpu.VMEM((QL, QL), BF),
            pltpu.VMEM((KVL, 2048), BF),
            pltpu.VMEM((HEADS, SUB, LAT), BF),
            pltpu.VMEM((2, 8, 96, TOK), BF),
            pltpu.VMEM((SLOTS, HEADS, SUB, LAT), BF),
            pltpu.VMEM((4, 4, 96, TOK), BF),
            pltpu.VMEM((HEADS, 2 * TOK, 2 * TOK), BF),
            pltpu.VMEM((PAIRS, 2 * TOK, TOK), BF),
            pltpu.VMEM((PAIRS, KEYS, 512), BF),
            pltpu.VMEM((2, KEYS, 2 * TOK), F32),
            pltpu.VMEM((KEYS, 2 * TOK), F32),
            pltpu.VMEM((2, KEYS, 2 * TOK), BF),
            pltpu.VMEM((KEYS, TOK), F32),
            pltpu.VMEM((2, TOK, 2 * TOK), F32),
            pltpu.VMEM((PAIRS, 4, TOK, 384), BF),
            pltpu.VMEM((PAIRS, 4, 2, 48, 384), BF),
            pltpu.VMEM((PAIRS, 4, 2, 48, 384), BF),
            pltpu.VMEM((HEADS, SUB, QL), BF),
            pltpu.VMEM((HEADS, SUB, QL), BF),
            pltpu.VMEM((SUB, QL), BF),
            pltpu.VMEM((SLOTS, HEADS, SUB, LAT), BF),
            pltpu.VMEM((HEADS, SLOTS, SUB, LAT), BF),
            pltpu.VMEM((SLOTS, SUB, LAT), BF),
            pltpu.VMEM((SLOTS, SUB, LAT), BF),
            dma((2,)),
            dma((SLOTS,)), dma((SLOTS,)),
            dma((PARTS, HEADS)), dma((PARTS, HEADS)),
            dma((3, 4)), dma((3, 4)),
            dma((PAIRS, 3)), dma((PAIRS, 3)),
            dma((PAIRS, 8)), dma((PAIRS, 8)),
            dma((HEADS,)), dma((HEADS,)),
            dma((HEADS,)), dma((HEADS,)),
            dma((PARTS, HEADS)), dma((PARTS, HEADS)),
            dma((SLOTS,)), dma((SLOTS,)),
        ],
        compiler_params=pltpu.CompilerParams(
            collective_id=0, has_side_effects=True, vmem_limit_bytes=VMEM_LIMIT
        ),
        name="attention_backward",
    )(x, kv, wq, wkv, do, trig, positions)


def shards(query_latent, kv_latent, query_up, kv_up, out_grad, positions):
    s = lax.axis_index("seq")
    local_positions = lax.dynamic_slice_in_dim(positions[0], s * TOK, TOK)
    half = ROPE // 2
    rates = 10000.0 ** (-jnp.arange(half, dtype=F32) / half)
    angles = local_positions.astype(F32)[:, None] * rates[None, :]
    trig = jnp.concatenate([jnp.cos(angles), jnp.sin(angles)], 1)
    query_grad, weight_grad, latent_grad = backward_pass(
        query_latent[0], kv_latent[0], query_up, kv_up, out_grad[0], trig, positions
    )
    return query_grad.reshape(1, TOK, QL), latent_grad[None], weight_grad


def solution(mesh):
    return jax.shard_map(
        shards,
        mesh=mesh,
        in_specs=(
            P("rep", "seq", None),
            P("rep", "seq", None),
            P(None, "head"),
            P(None, "head"),
            P("rep", "seq", "head"),
            P("rep", None),
        ),
        out_specs=(
            P("rep", "seq", None),
            P("rep", ("seq", "head"), None),
            P(("rep", "seq"), "head"),
        ),
        check_vma=False,
    )
```

```python
import jax
import jax.numpy as jnp
from jax import lax
from jax.experimental import pallas as pl
from jax.experimental.pallas import tpu as pltpu
from jax.sharding import PartitionSpec as P

QL = 1536
KVL = 512
ROPE = 64
NOPE = 128
VD = 128
HEADS = 8
TOK = 128
SLOTS = 12
SUB = 16
LAT = 640
KEYS = SLOTS * TOK
FIRST = 12
BF = jnp.bfloat16
F32 = jnp.float32
MESH = pl.DeviceIdType.MESH
VMEM_LIMIT = 63 * 1024 * 1024


def place():
    return lax.axis_index("rep"), lax.axis_index("seq"), lax.axis_index("head")


def group_base(s):
    return jnp.where(s < FIRST, 0, FIRST)


def z_partner(s):
    return s + 2 - 4 * lax.rem(lax.div(s, 2), 2)


def peer_rows(s):
    return lax.rem(lax.div(s, 2), 2)


def member(r, zb, yh):
    return 4 * r + 2 * zb + yh


def covered(z, zb, j):
    return lax.rem(jnp.where(zb == 0, z - j + 8, z + j), 8)


def remote(src, dst, send, recv, device):
    return pltpu.make_async_remote_copy(
        src_ref=src, dst_ref=dst, send_sem=send, recv_sem=recv, device_id=device, device_id_type=MESH
    )


def window(z, zb):
    return jnp.where(zb == 0, lax.rem(z + 5, 8), z)


def source_z(z, j):
    down = lax.rem(z + j, 8)
    up = lax.rem(z - j + 8, 8)
    return jnp.where(lax.rem(down, 2) == 0, down, up)


NT = (((1,), (1,)), ((), ()))
TN = (((0,), (0,)), ((), ()))
NN = (((1,), (0,)), ((), ()))
PAIRS = HEADS // 2
PARTS = 3
CHUNK = KEYS // PARTS
ROWS = 128


def dot(a, b, dims):
    return lax.dot_general(a, b, dims, preferred_element_type=F32)


def swap_halves(v):
    lane = lax.broadcasted_iota(jnp.int32, v.shape, 1)
    half = ROPE // 2
    return jnp.where(lax.rem(lane, ROPE) < half, pltpu.roll(v, TOK - half, 1), pltpu.roll(v, half, 1))


TURNS = [(dr, dz, dy) for dr in range(2) for dz in range(2) for dy in range(2)][1:]
MEMBERS = 8
REACH = 4


def kernel(
    x_ref, kv_ref, wq_hbm, wkv_hbm, do_ref, trig_ref, pos_ref,
    qg_ref, w_ref, l_ref,
    wq_v, wkv_v, kvx_s, xt_s, lat_s, xg_s, a_s, r_s, kvd_s, sp_s, sr_s, dp_s, rope_s, acc_s,
    dg_s, wp_s, rw_s, qt_s, rq_s, qs_s, dl_s, rl_s, ts_s, ry_s, ls_s, rlat_s,
    load, s1, r1, s2, r2, sx, rx, sdq, rdq, sw, rw, sqt, rqt, sqa, rqa, sdl, rdl, sls, rls,
):
    r, s, h = place()
    big = s < FIRST
    base = group_base(s)
    slot = s - base
    members = jnp.where(big, SLOTS, 4)
    part = lax.div(slot, 4)
    parts = part + 1
    z, zb, yh = lax.div(s, 2), peer_rows(s), lax.rem(s, 2)
    other = z_partner(s)
    mine = member(r, zb, yh)
    across = lax.rem(yh + 1, 2) - yh
    sibling, partner, far = (1 - r, s, h), (r, other, h), (r, s + across, h)
    plane = [lax.rem(h + d, HEADS) for d in range(1, HEADS)]
    circle = [(lax.rem(r + dr, 2), (other if dz else s) + across * dy, h) for dr, dz, dy in TURNS]
    owners = [(r, 2 * covered(z, zb, d) + yh, h) for d in range(REACH)]
    sources = [(r, 2 * source_z(z, d) + yh, h) for d in range(REACH)]

    barrier = pltpu.get_barrier_semaphore()

    def signal(device):
        pl.semaphore_signal(barrier, inc=1, device_id=device, device_id_type=MESH)

    for peer in plane:
        signal((r, s, peer))
    for device in circle:
        signal(device)
    for device in sources[1:]:
        signal(device)
    for k in range(SLOTS):
        @pl.when((k != slot) & (k < members))
        def _():
            signal((r, base + k, h))

    loads = [
        pltpu.make_async_copy(wq_hbm, wq_v, load.at[0]),
        pltpu.make_async_copy(wkv_hbm, wkv_v, load.at[1]),
    ]
    for copy in loads:
        copy.start()
    kvx_s[...] = jnp.concatenate([kv_ref[...], kv_ref[KVL:, :]], 0).T.reshape(HEADS, SUB, LAT)
    lat_s[slot, h] = kvx_s[h]
    pl.semaphore_wait(barrier, members - 1 + 17)

    def to_seq(k):
        return remote(kvx_s.at[h], lat_s.at[slot, h], s1.at[k], r1.at[slot], (r, base + k, h))

    def from_seq(k):
        return remote(kvx_s.at[h], lat_s.at[k, h], s1.at[k], r1.at[k], (r, base + k, h))

    def fresh(k):
        return (k != slot) & (k < members) & (k // 4 >= part)

    def older(k):
        return (k != slot) & (k < members) & ((k // 4 if isinstance(k, int) else lax.div(k, 4)) <= part)

    for k in range(SLOTS):
        @pl.when(fresh(k))
        def _():
            to_seq(k).start()

    def columns(k):
        dr, dz, dy = TURNS[k]
        pr, pzb, py = lax.rem(r + dr, 2), lax.rem(zb + dz, 2), lax.rem(yh + dy, 2)
        start = window(lax.div(other if dz else s, 2), pzb)
        return remote(xt_s.at[pr, pl.ds(start, REACH), py], xg_s.at[mine], sx.at[k], rx.at[k], circle[k])

    def slots_of(p):
        return pl.ds(pl.multiple_of(4 * p, 4), 4)

    def to_plane(p, d):
        return remote(
            lat_s.at[slots_of(p), h], lat_s.at[slots_of(p), h], s2.at[p, d], r2.at[p, d], (r, s, plane[d - 1])
        )

    def from_plane(p, d):
        source = lax.rem(h - d + HEADS, HEADS)
        return remote(
            lat_s.at[slots_of(p), h], lat_s.at[slots_of(p), source], s2.at[p, d], r2.at[p, d], (r, s, source)
        )

    scale = (NOPE + ROPE) ** (-0.5)
    cosine = jnp.concatenate([trig_ref[:, : ROPE // 2]] * 4, 1)
    sine = jnp.concatenate([-trig_ref[:, ROPE // 2 :], trig_ref[:, ROPE // 2 :]] * 2, 1)
    left = lax.broadcasted_iota(jnp.int32, (TOK, TOK), 1) < ROPE
    loads[0].wait()
    for g in range(PAIRS):
        projected = dot(x_ref[...], wq_v[:, 384 * g : 384 * (g + 1)], NN)
        one, mid, last = (projected[:, TOK * k : TOK * (k + 1)] for k in range(3))
        two = jnp.where(left, pltpu.roll(mid, ROPE, 1), pltpu.roll(last, ROPE, 1))
        none = jnp.zeros((TOK, TOK), BF)
        for k, nope in enumerate((one, two)):
            i = 2 * g + k
            a_s[i, :TOK, :TOK] = nope.astype(BF)
            a_s[i, :TOK, TOK:] = none
            a_s[i, TOK:, :TOK] = none
            a_s[i, TOK:, TOK:] = do_ref[:, TOK * i : TOK * (i + 1)]
        r_s[g, :TOK, :] = jnp.where(left, mid * cosine + swap_halves(mid) * sine, 0.0).astype(BF)
        r_s[g, TOK:, :] = jnp.where(left, 0.0, last * cosine + swap_halves(last) * sine).astype(BF)
    rope_s[...] = jnp.zeros_like(rope_s)
    def share(i, nothing):
        p = part - i
        for k in range(4):
            @pl.when(older(4 * p + k))
            def _():
                from_seq(4 * p + k).wait_recv()
        for d in range(1, HEADS):
            to_plane(p, d).start()
        return nothing

    lax.fori_loop(0, parts, share, 0)
    turned = x_ref[...].T.reshape(2, 8, 2, 48, TOK)
    xt_s[:, :8] = turned
    xt_s[:, 8:] = turned
    for k in range(7):
        columns(k).start()
    xg_s[mine] = xt_s[r, pl.ds(window(z, zb), REACH), yh]
    loads[1].wait()

    def chunk_at(p):
        return pl.ds(pl.multiple_of(p * CHUNK, CHUNK), CHUNK)

    def latent_chunk(p):
        return lat_s[slots_of(p)].reshape(CHUNK, LAT)

    def keys_of(i, nothing):
        p = part - i
        for d in range(1, HEADS):
            from_plane(p, d).wait_recv()
        rows = latent_chunk(p)[:, :KVL]
        for g in range(PAIRS):
            kvd_s[g, chunk_at(p), :] = dot(rows, wkv_v[:, 512 * g : 512 * (g + 1)], NN).astype(BF)
        return nothing

    lax.fori_loop(0, parts, keys_of, 0)
    first_row = pl.ds(pl.multiple_of(s * TOK, TOK), TOK)
    high = slot * TOK + lax.broadcasted_iota(jnp.int32, (1, TOK), 1)
    low = high - pos_ref[:, first_row]
    steps = parts * (CHUNK // ROWS)
    fold = (ROWS // 8, 8, TOK)
    both = range(2)

    routes = [
        (0, 0, sibling), (0, 0, partner), (0, 0, far), (1, 0, sibling), (1, 0, far), (0, 1, sibling), (1, 1, sibling)
    ]
    arrivals = [(1, 0, 0), (0, 1, 0), (0, 0, 1), (1, 1, 0), (0, 1, 1), (1, 0, 1), (1, 1, 1)]

    def turn(dr, dz, dy):
        return member(lax.rem(r + dr, 2), lax.rem(zb + dz, 2), lax.rem(yh + dy, 2))

    def hand_out(g, k):
        dz, dy, device = routes[k]
        block = dg_s.at[g, turn(0, dz, dy)]
        return remote(block, block, sdq.at[g, k], rdq.at[g, k], device)

    def hand_in(g, k):
        block = dg_s.at[g, turn(*arrivals[k])]
        return remote(block, block, sdq.at[g, k], rdq.at[g, k], sibling)

    def relay(g, arrived, onward):
        hand_in(g, arrived).wait_recv()
        for k in onward:
            hand_out(g, k).start()

    def relay_z(g):
        relay(g, 1, (4, 3))

    def relay_y(g):
        relay(g, 2, (5,))

    def relay_zy(g):
        relay(g, 4, (6,))

    def piece(d):
        return jnp.where(zb == 0, REACH - 1 - d, d)

    def to_owner(g, d):
        return remote(wp_s.at[g, piece(d)], rw_s.at[g, d], sw.at[g, d], rw.at[g, d], owners[d])

    def from_source(g, d):
        return remote(wp_s.at[g, 0], rw_s.at[g, d], sw.at[g, d], rw.at[g, d], sources[d])

    def weights(g):
        for k in (0, 3, 5, 6):
            hand_in(g, k).wait_recv()
        rows = jnp.concatenate([xg_s[k].reshape(REACH * 48, TOK) for k in range(MEMBERS)], 1)
        product = dot(rows, dg_s[g].reshape(MEMBERS * TOK, 384), NN)
        wp_s[g] = product.astype(BF).reshape(REACH, 48, 384)
        for d in (3, 2, 1):
            to_owner(g, d).start()

    def pair(g, carry):
        def scores(p, nothing):
            at = chunk_at(p)
            for k in both:
                sp_s[k, at, :] = dot(kvd_s[g, at, 256 * k : 256 * (k + 1)], a_s[2 * g + k], NT)
            sr_s[at, :] = dot(latent_chunk(p)[:, KVL:], r_s[g], NT)
            return nothing

        lax.fori_loop(0, parts, scores, 0)

        def first(c, tops):
            at = pl.ds(pl.multiple_of(c * ROWS, ROWS), ROWS)
            key = c * ROWS + lax.broadcasted_iota(jnp.int32, (ROWS, TOK), 0)
            seen = (key >= low) & (key <= high)
            out = []
            for k in both:
                value = (sp_s[k, at, :TOK] + sr_s[at, TOK * k : TOK * (k + 1)]) * scale
                value = jnp.where(seen, value, -jnp.inf)
                sp_s[k, at, :TOK] = value
                out.append(jnp.maximum(tops[k], jnp.max(value.reshape(fold), 0)))
            return tuple(out)

        start = jnp.full((8, TOK), -jnp.inf, F32)
        tops = lax.fori_loop(0, steps, first, (start, start))
        tops = [jnp.max(top, 0, keepdims=True) for top in tops]

        def second(c, sums):
            at = pl.ds(pl.multiple_of(c * ROWS, ROWS), ROWS)
            out = []
            for k in both:
                value = jnp.exp(sp_s[k, at, :TOK] - tops[k])
                sp_s[k, at, :TOK] = value
                out.append(sums[2 * k] + jnp.sum(value.reshape(fold), 0))
                out.append(sums[2 * k + 1] + jnp.sum((value * sp_s[k, at, TOK:]).reshape(fold), 0))
            return tuple(out)

        zero = jnp.zeros((8, TOK), F32)
        sums = lax.fori_loop(0, steps, second, (zero,) * 4)
        inverse = [1.0 / jnp.sum(sums[2 * k], 0, keepdims=True) for k in both]
        inner = [jnp.sum(sums[2 * k + 1], 0, keepdims=True) * inverse[k] for k in both]

        @pl.when(g >= 1)
        def _():
            relay_z(g - 1)

        @pl.when(g >= 2)
        def _():
            relay_zy(g - 2)

        def third(c, nothing):
            at = pl.ds(pl.multiple_of(c * ROWS, ROWS), ROWS)
            for k in both:
                weight = sp_s[k, at, :TOK] * inverse[k]
                dp_s[k, at, TOK:] = weight.astype(BF)
                dp_s[k, at, :TOK] = (weight * (sp_s[k, at, TOK:] - inner[k]) * scale).astype(BF)
            return nothing

        lax.fori_loop(0, steps, third, 0)
        acc_s[...] = jnp.zeros_like(acc_s)

        def backward(p, nothing):
            at = chunk_at(p)
            key_rope = latent_chunk(p)[:, KVL:]
            for k in both:
                score_grad = dp_s[k, at, :TOK]
                rows = jnp.concatenate([kvd_s[g, at, 256 * k : 256 * k + NOPE], key_rope], 1)
                acc_s[k] += dot(score_grad, rows, TN)
                kvd_s[g, at, 256 * k : 256 * (k + 1)] = dot(dp_s[k, at, :], a_s[2 * g + k], NN).astype(BF)
            grads = jnp.concatenate([dp_s[0, at, :TOK], dp_s[1, at, :TOK]], 1)
            rope_s[at, :] += dot(grads, r_s[g], NN).astype(BF).astype(F32)
            return nothing

        lax.fori_loop(0, parts, backward, 0)
        ropes = []
        for k in both:
            chunk = acc_s[k, :, TOK:]
            ropes.append(chunk * cosine - swap_halves(chunk) * sine)
        second_nope = pltpu.roll(acc_s[1, :, :TOK], ROPE, 1)
        dg_s[g, mine] = jnp.concatenate(
            [acc_s[0, :, :TOK], jnp.where(left, ropes[0], second_nope), jnp.where(left, second_nope, ropes[1])], 1
        ).astype(BF)
        for k in (1, 2, 0):
            hand_out(g, k).start()

        @pl.when(g >= 1)
        def _():
            relay_y(g - 1)

        @pl.when(g == 2)
        def _():
            for k, (dr, dz, dy) in enumerate(TURNS):
                remote(xg_s.at[mine], xg_s.at[turn(dr, dz, dy)], sx.at[k], rx.at[k], sibling).wait_recv()

        @pl.when(g >= 2)
        def _():
            weights(g - 2)

        return carry

    lax.fori_loop(0, PAIRS, pair, 0)

    joined = jnp.concatenate([dg_s[g, mine] for g in range(PAIRS)], 1)
    qt_s[...] = dot(joined, wq_v[...], NT).astype(BF).reshape(HEADS, SUB, QL)

    def query_out(d):
        return remote(qt_s.at[plane[d - 1]], rq_s.at[h], sqt.at[d], rqt.at[d], (r, s, plane[d - 1]))

    for d in range(1, HEADS):
        query_out(d).start()

    row, column = lax.div(h, 4), lax.rem(h, 4)

    def latent_out(p, d):
        to = lax.rem(column + d, 4)
        return remote(
            dl_s.at[slots_of(p), :, to], rl_s.at[column, slots_of(p)], sdl.at[p, d], rdl.at[p, d],
            (r, s, 4 * row + to),
        )

    def latent_in(p, d):
        source = lax.rem(column - d + 4, 4)
        return remote(
            dl_s.at[slots_of(p), :, column], rl_s.at[source, slots_of(p)], sdl.at[p, d], rdl.at[p, d],
            (r, s, 4 * row + source),
        )

    def latent_cross(p):
        return remote(
            ts_s.at[slots_of(p), 1 - row], ry_s.at[slots_of(p)], sdl.at[p, 0], rdl.at[p, 0],
            (r, s, 4 * (1 - row) + column),
        )

    def latents(p):
        at = chunk_at(p)
        rows = jnp.concatenate([kvd_s[g, at, :] for g in range(PAIRS)], 1)
        low_part = dot(rows, wkv_v[...], NT).astype(BF)
        rope = rope_s[at, :]
        rope = (rope + pltpu.roll(rope, ROPE, 1)).astype(BF)
        dl_s[slots_of(p)] = jnp.concatenate([low_part, rope], 1).reshape(4, 2, 4, SUB, LAT)
        for d in range(1, 4):
            latent_out(p, d).start()

    latents(0)
    relay_z(PAIRS - 1)
    relay_zy(PAIRS - 2)

    @pl.when(parts > 1)
    def _():
        latents(1)

    relay_y(PAIRS - 1)
    weights(PAIRS - 2)

    @pl.when(parts > 2)
    def _():
        latents(2)

    relay_zy(PAIRS - 1)
    weights(PAIRS - 1)

    total = qt_s[h].astype(F32)
    for d in range(1, HEADS):
        source = lax.rem(h - d + HEADS, HEADS)
        remote(qt_s.at[h], rq_s.at[source], sqt.at[d], rqt.at[d], (r, s, source)).wait_recv()
        total += rq_s[source].astype(F32)
    qs_s[...] = total.astype(BF)
    qg_ref[h] = qs_s[...]

    def query_share(d):
        return remote(qs_s, qg_ref.at[h], sqa.at[d], rqa.at[d], (r, s, plane[d - 1]))

    for d in range(1, HEADS):
        query_share(d).start()

    def to_latent_owner(k):
        return remote(ls_s.at[k], rlat_s.at[slot], sls.at[k], rls.at[slot], (r, base + k, h))

    def from_latent_source(k):
        return remote(ls_s.at[k], rlat_s.at[k], sls.at[k], rls.at[k], (r, base + k, h))

    def add_row(p):
        for d in range(1, 4):
            latent_in(p, d).wait_recv()
        for k in range(4 * p, 4 * p + 4):
            total = dl_s[k, :, column].astype(F32)
            for d in range(1, 4):
                total += rl_s[lax.rem(column + d, 4), k].astype(F32)
            ts_s[k] = total.astype(BF)
        latent_cross(p).start()

    def add_column(p):
        latent_cross(p).wait_recv()
        for k in range(4 * p, 4 * p + 4):
            ls_s[k] = (ts_s[k, row].astype(F32) + ry_s[k].astype(F32)).astype(BF)

            @pl.when(older(k))
            def _():
                to_latent_owner(k).start()

    add_row(0)
    for p in range(1, PARTS):
        @pl.when(p < parts)
        def _():
            add_row(p)

        add_column(p - 1) if p == 1 else pl.when(p - 1 < parts)(lambda: add_column(p - 1))

    pl.when(PARTS - 1 < parts)(lambda: add_column(PARTS - 1))

    for g in range(PAIRS):
        total = wp_s[g, piece(0)].astype(F32)
        for d in range(1, REACH):
            from_source(g, d).wait_recv()
            total += rw_s[g, d].astype(F32)
        w_ref[:, 384 * g : 384 * (g + 1)] = total.astype(BF)

    acc_s[0, :SUB, :] = ls_s[slot, :, :256].astype(F32)
    acc_s[0, SUB : 2 * SUB, :] = ls_s[slot, :, 256:512].astype(F32)
    acc_s[0, 2 * SUB : 3 * SUB, :TOK] = ls_s[slot, :, 512:].astype(F32)
    for k in range(SLOTS):
        @pl.when(fresh(k))
        def _():
            from_latent_source(k).wait_recv()
            acc_s[0, :SUB, :] += rlat_s[k, :, :256].astype(F32)
            acc_s[0, SUB : 2 * SUB, :] += rlat_s[k, :, 256:512].astype(F32)
            acc_s[0, 2 * SUB : 3 * SUB, :TOK] += rlat_s[k, :, 512:].astype(F32)
    l_ref[...] = jnp.concatenate(
        [acc_s[0, :SUB, :], acc_s[0, SUB : 2 * SUB, :], acc_s[0, 2 * SUB : 3 * SUB, :ROPE]], 1
    ).astype(BF)

    for d in range(1, HEADS):
        source = lax.rem(h - d + HEADS, HEADS)
        remote(qs_s, qg_ref.at[source], sqa.at[d], rqa.at[d], (r, s, source)).wait_recv()
        query_share(d).wait_send()
        query_out(d).wait_send()
    for k in range(SLOTS):
        @pl.when(fresh(k))
        def _():
            to_seq(k).wait_send()

        @pl.when(older(k))
        def _():
            to_latent_owner(k).wait_send()
    for k in range(7):
        columns(k).wait_send()

    def drain_part(p, nothing):
        for d in range(1, HEADS):
            to_plane(p, d).wait_send()
        for d in range(1, 4):
            latent_out(p, d).wait_send()
        latent_cross(p).wait_send()
        return nothing

    lax.fori_loop(0, parts, drain_part, 0)

    def drain_pair(g, nothing):
        for k in range(7):
            hand_out(g, k).wait_send()
        for d in range(1, REACH):
            to_owner(g, d).wait_send()
        return nothing

    lax.fori_loop(0, PAIRS, drain_pair, 0)


def backward_pass(x, kv, wq, wkv, do, trig, positions):
    dma = pltpu.SemaphoreType.DMA
    vmem = pl.BlockSpec(memory_space=pltpu.VMEM)
    hbm = pl.BlockSpec(memory_space=pl.ANY)
    return pl.pallas_call(
        kernel,
        out_shape=(
            jax.ShapeDtypeStruct((HEADS, SUB, QL), BF),
            jax.ShapeDtypeStruct((48, QL), BF),
            jax.ShapeDtypeStruct((SUB, KVL + ROPE), BF),
        ),
        in_specs=[vmem, vmem, hbm, hbm, vmem, vmem, vmem],
        out_specs=(vmem,) * 3,
        scratch_shapes=[
            pltpu.VMEM((QL, QL), BF),
            pltpu.VMEM((KVL, 2048), BF),
            pltpu.VMEM((HEADS, SUB, LAT), BF),
            pltpu.VMEM((2, 16, 2, 48, TOK), BF),
            pltpu.VMEM((SLOTS, HEADS, SUB, LAT), BF),
            pltpu.VMEM((MEMBERS, REACH, 48, TOK), BF),
            pltpu.VMEM((HEADS, 2 * TOK, 2 * TOK), BF),
            pltpu.VMEM((PAIRS, 2 * TOK, TOK), BF),
            pltpu.VMEM((PAIRS, KEYS, 512), BF),
            pltpu.VMEM((2, KEYS, 2 * TOK), F32),
            pltpu.VMEM((KEYS, 2 * TOK), F32),
            pltpu.VMEM((2, KEYS, 2 * TOK), BF),
            pltpu.VMEM((KEYS, TOK), F32),
            pltpu.VMEM((2, TOK, 2 * TOK), F32),
            pltpu.VMEM((PAIRS, MEMBERS, TOK, 384), BF),
            pltpu.VMEM((PAIRS, REACH, 48, 384), BF),
            pltpu.VMEM((PAIRS, REACH, 48, 384), BF),
            pltpu.VMEM((HEADS, SUB, QL), BF),
            pltpu.VMEM((HEADS, SUB, QL), BF),
            pltpu.VMEM((SUB, QL), BF),
            pltpu.VMEM((SLOTS, 2, 4, SUB, LAT), BF),
            pltpu.VMEM((4, SLOTS, 2, SUB, LAT), BF),
            pltpu.VMEM((SLOTS, 2, SUB, LAT), BF),
            pltpu.VMEM((SLOTS, SUB, LAT), BF),
            pltpu.VMEM((SLOTS, SUB, LAT), BF),
            pltpu.VMEM((SLOTS, SUB, LAT), BF),
            dma((2,)),
            dma((SLOTS,)), dma((SLOTS,)),
            dma((PARTS, HEADS)), dma((PARTS, HEADS)),
            dma((7,)), dma((7,)),
            dma((PAIRS, 7)), dma((PAIRS, 7)),
            dma((PAIRS, REACH)), dma((PAIRS, REACH)),
            dma((HEADS,)), dma((HEADS,)),
            dma((HEADS,)), dma((HEADS,)),
            dma((PARTS, HEADS)), dma((PARTS, HEADS)),
            dma((SLOTS,)), dma((SLOTS,)),
        ],
        compiler_params=pltpu.CompilerParams(
            collective_id=0, has_side_effects=True, vmem_limit_bytes=VMEM_LIMIT
        ),
        name="attention_backward",
    )(x, kv, wq, wkv, do, trig, positions)


def hand_over_kernel(*refs):
    for source, target in zip(refs[:3], refs[3:]):
        target[...] = source[...]


def hand_over(*arrays):
    vmem = pl.BlockSpec(memory_space=pltpu.VMEM)
    return pl.pallas_call(
        hand_over_kernel,
        out_shape=tuple(jax.ShapeDtypeStruct(a.shape, a.dtype) for a in arrays),
        in_specs=[vmem] * 3,
        out_specs=(vmem,) * 3,
        name="hand_over",
    )(*arrays)


def shards(query_latent, kv_latent, query_up, kv_up, out_grad, positions):
    s = lax.axis_index("seq")
    local_positions = lax.dynamic_slice_in_dim(positions[0], s * TOK, TOK)
    half = ROPE // 2
    lane = jnp.arange(ROPE)
    rates = 10000.0 ** (-(lane % half).astype(F32) / half)
    angles = local_positions.astype(F32)[:, None] * rates[None, :]
    trig = jnp.where(lane[None, :] < half, jnp.cos(angles), jnp.sin(angles))
    query_grad, weight_grad, latent_grad = backward_pass(
        query_latent[0], kv_latent[0].T, query_up, kv_up, out_grad[0], trig, positions
    )
    query_grad, weight_grad, latent_grad = hand_over(query_grad, weight_grad, latent_grad)
    return query_grad.reshape(1, TOK, QL), latent_grad[None], weight_grad


def solution(mesh):
    return jax.shard_map(
        shards,
        mesh=mesh,
        in_specs=(
            P("rep", "seq", None),
            P("rep", "seq", None),
            P(None, "head"),
            P(None, "head"),
            P("rep", "seq", "head"),
            P("rep", None),
        ),
        out_specs=(
            P("rep", "seq", None),
            P("rep", ("seq", "head"), None),
            P(("rep", "seq"), "head"),
        ),
        check_vma=False,
    )
```

```python
import jax
import jax.numpy as jnp
from jax import lax
from jax.experimental import pallas as pl
from jax.experimental.pallas import tpu as pltpu
from jax.sharding import PartitionSpec as P

QL = 1536
KVL = 512
ROPE = 64
NOPE = 128
VD = 128
HEADS = 8
TOK = 128
SLOTS = 12
SUB = 16
LAT = 640
KEYS = SLOTS * TOK
FIRST = 12
BF = jnp.bfloat16
F32 = jnp.float32
MESH = pl.DeviceIdType.MESH
VMEM_LIMIT = 63 * 1024 * 1024


def place():
    return lax.axis_index("rep"), lax.axis_index("seq"), lax.axis_index("head")


def group_base(s):
    return jnp.where(s < FIRST, 0, FIRST)


def z_partner(s):
    return s + 2 - 4 * lax.rem(lax.div(s, 2), 2)


def peer_rows(s):
    return lax.rem(lax.div(s, 2), 2)


def member(r, zb, yh):
    return 4 * r + 2 * zb + yh


def covered(z, zb, j):
    return lax.rem(jnp.where(zb == 0, z - j + 8, z + j), 8)


def remote(src, dst, send, recv, device):
    return pltpu.make_async_remote_copy(
        src_ref=src, dst_ref=dst, send_sem=send, recv_sem=recv, device_id=device, device_id_type=MESH
    )


def window(z, zb):
    return jnp.where(zb == 0, lax.rem(z + 5, 8), z)


def source_z(z, j):
    down = lax.rem(z + j, 8)
    up = lax.rem(z - j + 8, 8)
    return jnp.where(lax.rem(down, 2) == 0, down, up)


NT = (((1,), (1,)), ((), ()))
TN = (((0,), (0,)), ((), ()))
NN = (((1,), (0,)), ((), ()))
PAIRS = HEADS // 2
PARTS = 3
CHUNK = KEYS // PARTS
ROWS = 128


def dot(a, b, dims):
    return lax.dot_general(a, b, dims, preferred_element_type=F32)


def swap_halves(v):
    lane = lax.broadcasted_iota(jnp.int32, v.shape, 1)
    half = ROPE // 2
    return jnp.where(lax.rem(lane, ROPE) < half, pltpu.roll(v, TOK - half, 1), pltpu.roll(v, half, 1))


TURNS = [(dr, dz, dy) for dr in range(2) for dz in range(2) for dy in range(2)][1:]
MEMBERS = 8
REACH = 4


def kernel(
    x_ref, kv_ref, wq_hbm, wkv_hbm, do_ref, trig_ref, pos_ref,
    qg_ref, w_ref, l_ref,
    wq_v, wkv_v, kvx_s, xt_s, lat_s, xg_s, a_s, r_s, kvd_s, sp_s, sr_s, dp_s, rope_s, acc_s,
    dg_s, wp_s, rw_s, qt_s, rq_s, qs_s, dl_s, rl_s, ts_s, ry_s, rb_s, tb_s, rx_s, ls_s, rlat_s,
    load, s1, r1, s2, r2, sx, rx, sdq, rdq, sw, rw, sqt, rqt, sqa, rqa, sdl, rdl, sls, rls,
):
    r, s, h = place()
    big = s < FIRST
    base = group_base(s)
    slot = s - base
    members = jnp.where(big, SLOTS, 4)
    part = lax.div(slot, 4)
    parts = part + 1
    z, zb, yh = lax.div(s, 2), peer_rows(s), lax.rem(s, 2)
    other = z_partner(s)
    mine = member(r, zb, yh)
    across = lax.rem(yh + 1, 2) - yh
    sibling, partner, far = (1 - r, s, h), (r, other, h), (r, s + across, h)
    plane = [lax.rem(h + d, HEADS) for d in range(1, HEADS)]
    circle = [(lax.rem(r + dr, 2), (other if dz else s) + across * dy, h) for dr, dz, dy in TURNS]
    owners = [(r, 2 * covered(z, zb, d) + yh, h) for d in range(REACH)]
    sources = [(r, 2 * source_z(z, d) + yh, h) for d in range(REACH)]

    barrier = pltpu.get_barrier_semaphore()

    def signal(device):
        pl.semaphore_signal(barrier, inc=1, device_id=device, device_id_type=MESH)

    for peer in plane:
        signal((r, s, peer))
    for device in circle:
        signal(device)
    for device in sources[1:]:
        signal(device)
    for k in range(SLOTS):
        @pl.when((k != slot) & (k < members))
        def _():
            signal((r, base + k, h))

    loads = [
        pltpu.make_async_copy(wq_hbm, wq_v, load.at[0]),
        pltpu.make_async_copy(wkv_hbm, wkv_v, load.at[1]),
    ]
    for copy in loads:
        copy.start()
    kvx_s[...] = jnp.concatenate([kv_ref[...], kv_ref[KVL:, :]], 0).T.reshape(HEADS, SUB, LAT)
    lat_s[slot, h] = kvx_s[h]
    pl.semaphore_wait(barrier, members - 1 + 17)

    def to_seq(k):
        return remote(kvx_s.at[h], lat_s.at[slot, h], s1.at[k], r1.at[slot], (r, base + k, h))

    def from_seq(k):
        return remote(kvx_s.at[h], lat_s.at[k, h], s1.at[k], r1.at[k], (r, base + k, h))

    def fresh(k):
        return (k != slot) & (k < members) & (k // 4 >= part)

    def older(k):
        return (k != slot) & (k < members) & ((k // 4 if isinstance(k, int) else lax.div(k, 4)) <= part)

    for k in range(SLOTS):
        @pl.when(fresh(k))
        def _():
            to_seq(k).start()

    def columns(k):
        dr, dz, dy = TURNS[k]
        pr, pzb, py = lax.rem(r + dr, 2), lax.rem(zb + dz, 2), lax.rem(yh + dy, 2)
        start = window(lax.div(other if dz else s, 2), pzb)
        return remote(xt_s.at[pr, pl.ds(start, REACH), py], xg_s.at[mine], sx.at[k], rx.at[k], circle[k])

    def slots_of(p):
        return pl.ds(pl.multiple_of(4 * p, 4), 4)

    row, column = lax.div(h, 4), lax.rem(h, 4)

    def early(p):
        return pl.ds(pl.multiple_of(4 * p, 2), 2)

    def late(p):
        return pl.ds(pl.multiple_of(4 * p + 2, 2), 2)

    def beside(d):
        return lax.rem(column + d, 4)

    def in_row(d):
        return (r, s, 4 * row + beside(d))

    opposite = (r, s, 4 * (1 - row) + column)

    def behind(d):
        return lax.rem(column - d + 4, 4)

    def block(at, heads, to, p, n):
        ref = lat_s.at[at, heads]
        return remote(ref, ref, s2.at[p, n], r2.at[p, n], to)

    turned_h = 4 * (1 - row) + column

    def share_y(p, h_from=None):
        return block(early(p), h if h_from is None else h_from, opposite, p, 0)

    def share_x(p, d, h_from=None):
        return block(early(p), h if h_from is None else h_from, in_row(d), p, d)

    def share_yx(p, d, h_from=None):
        return block(early(p), turned_h if h_from is None else h_from, in_row(d), p, 3 + d)

    def late_x(p, d, h_from=None):
        return block(late(p), h if h_from is None else h_from, in_row(d), p, 6 + d)

    def late_xy(p, from_row=None):
        at = pl.ds(pl.multiple_of(4 * (row if from_row is None else from_row), 4), 4)
        return block(late(p), at, opposite, p, 10)

    scale = (NOPE + ROPE) ** (-0.5)
    cosine = jnp.concatenate([trig_ref[:, : ROPE // 2]] * 4, 1)
    sine = jnp.concatenate([-trig_ref[:, ROPE // 2 :], trig_ref[:, ROPE // 2 :]] * 2, 1)
    left = lax.broadcasted_iota(jnp.int32, (TOK, TOK), 1) < ROPE
    loads[0].wait()
    for g in range(PAIRS):
        projected = dot(x_ref[...], wq_v[:, 384 * g : 384 * (g + 1)], NN)
        one, mid, last = (projected[:, TOK * k : TOK * (k + 1)] for k in range(3))
        two = jnp.where(left, pltpu.roll(mid, ROPE, 1), pltpu.roll(last, ROPE, 1))
        none = jnp.zeros((TOK, TOK), BF)
        for k, nope in enumerate((one, two)):
            i = 2 * g + k
            a_s[i, :TOK, :TOK] = nope.astype(BF)
            a_s[i, :TOK, TOK:] = none
            a_s[i, TOK:, :TOK] = none
            a_s[i, TOK:, TOK:] = do_ref[:, TOK * i : TOK * (i + 1)]
        r_s[g, :TOK, :] = jnp.where(left, mid * cosine + swap_halves(mid) * sine, 0.0).astype(BF)
        r_s[g, TOK:, :] = jnp.where(left, 0.0, last * cosine + swap_halves(last) * sine).astype(BF)
    rope_s[...] = jnp.zeros_like(rope_s)
    def share(i, nothing):
        p = part - i
        for k in range(4):
            @pl.when(older(4 * p + k))
            def _():
                from_seq(4 * p + k).wait_recv()
        share_y(p).start()
        for d in range(1, 4):
            late_x(p, d).start()
        for d in range(1, 4):
            share_x(p, d).start()

        @pl.when(i >= 1)
        def _():
            onward(p + 1)

        return nothing

    def onward(p):
        share_y(p, turned_h).wait_recv()
        for d in range(1, 4):
            share_yx(p, d).start()
        for d in range(1, 4):
            late_x(p, d, 4 * row + behind(d)).wait_recv()
        late_xy(p).start()

    lax.fori_loop(0, parts, share, 0)
    onward(0)
    turned = x_ref[...].T.reshape(2, 8, 2, 48, TOK)
    xt_s[:, :8] = turned
    xt_s[:, 8:] = turned
    for k in range(7):
        columns(k).start()
    xg_s[mine] = xt_s[r, pl.ds(window(z, zb), REACH), yh]
    loads[1].wait()

    def chunk_at(p):
        return pl.ds(pl.multiple_of(p * CHUNK, CHUNK), CHUNK)

    def latent_chunk(p):
        return lat_s[slots_of(p)].reshape(CHUNK, LAT)

    def keys_of(i, nothing):
        p = part - i
        for d in range(1, 4):
            share_x(p, d, 4 * row + behind(d)).wait_recv()
            share_yx(p, d, 4 * (1 - row) + behind(d)).wait_recv()
        late_xy(p, 1 - row).wait_recv()
        rows = latent_chunk(p)[:, :KVL]
        for g in range(PAIRS):
            kvd_s[g, chunk_at(p), :] = dot(rows, wkv_v[:, 512 * g : 512 * (g + 1)], NN).astype(BF)
        return nothing

    lax.fori_loop(0, parts, keys_of, 0)
    first_row = pl.ds(pl.multiple_of(s * TOK, TOK), TOK)
    high = slot * TOK + lax.broadcasted_iota(jnp.int32, (1, TOK), 1)
    low = high - pos_ref[:, first_row]
    steps = parts * (CHUNK // ROWS)
    fold = (ROWS // 8, 8, TOK)
    both = range(2)

    routes = [
        (0, 0, sibling), (0, 0, partner), (0, 0, far), (1, 0, sibling), (1, 0, far), (0, 1, sibling), (1, 1, sibling)
    ]
    arrivals = [(1, 0, 0), (0, 1, 0), (0, 0, 1), (1, 1, 0), (0, 1, 1), (1, 0, 1), (1, 1, 1)]

    def turn(dr, dz, dy):
        return member(lax.rem(r + dr, 2), lax.rem(zb + dz, 2), lax.rem(yh + dy, 2))

    def hand_out(g, k):
        dz, dy, device = routes[k]
        block = dg_s.at[g, turn(0, dz, dy)]
        return remote(block, block, sdq.at[g, k], rdq.at[g, k], device)

    def hand_in(g, k):
        block = dg_s.at[g, turn(*arrivals[k])]
        return remote(block, block, sdq.at[g, k], rdq.at[g, k], sibling)

    def relay(g, arrived, onward):
        hand_in(g, arrived).wait_recv()
        for k in onward:
            hand_out(g, k).start()

    def relay_z(g):
        relay(g, 1, (4, 3))

    def relay_y(g):
        relay(g, 2, (5,))

    def relay_zy(g):
        relay(g, 4, (6,))

    def piece(d):
        return jnp.where(zb == 0, REACH - 1 - d, d)

    def to_owner(g, d):
        return remote(wp_s.at[g, piece(d)], rw_s.at[g, d], sw.at[g, d], rw.at[g, d], owners[d])

    def from_source(g, d):
        return remote(wp_s.at[g, 0], rw_s.at[g, d], sw.at[g, d], rw.at[g, d], sources[d])

    def weights(g):
        for k in (0, 3, 5, 6):
            hand_in(g, k).wait_recv()
        rows = jnp.concatenate([xg_s[k].reshape(REACH * 48, TOK) for k in range(MEMBERS)], 1)
        product = dot(rows, dg_s[g].reshape(MEMBERS * TOK, 384), NN)
        wp_s[g] = product.astype(BF).reshape(REACH, 48, 384)
        for d in (3, 2, 1):
            to_owner(g, d).start()

    def pair(g, carry):
        def scores(p, nothing):
            at = chunk_at(p)
            for k in both:
                sp_s[k, at, :] = dot(kvd_s[g, at, 256 * k : 256 * (k + 1)], a_s[2 * g + k], NT)
            sr_s[at, :] = dot(latent_chunk(p)[:, KVL:], r_s[g], NT)
            return nothing

        lax.fori_loop(0, parts, scores, 0)

        def first(c, tops):
            at = pl.ds(pl.multiple_of(c * ROWS, ROWS), ROWS)
            key = c * ROWS + lax.broadcasted_iota(jnp.int32, (ROWS, TOK), 0)
            seen = (key >= low) & (key <= high)
            out = []
            for k in both:
                value = (sp_s[k, at, :TOK] + sr_s[at, TOK * k : TOK * (k + 1)]) * scale
                value = jnp.where(seen, value, -jnp.inf)
                sp_s[k, at, :TOK] = value
                out.append(jnp.maximum(tops[k], jnp.max(value.reshape(fold), 0)))
            return tuple(out)

        start = jnp.full((8, TOK), -jnp.inf, F32)
        tops = lax.fori_loop(0, steps, first, (start, start))
        tops = [jnp.max(top, 0, keepdims=True) for top in tops]

        def second(c, sums):
            at = pl.ds(pl.multiple_of(c * ROWS, ROWS), ROWS)
            out = []
            for k in both:
                value = jnp.exp(sp_s[k, at, :TOK] - tops[k])
                sp_s[k, at, :TOK] = value
                out.append(sums[2 * k] + jnp.sum(value.reshape(fold), 0))
                out.append(sums[2 * k + 1] + jnp.sum((value * sp_s[k, at, TOK:]).reshape(fold), 0))
            return tuple(out)

        zero = jnp.zeros((8, TOK), F32)
        sums = lax.fori_loop(0, steps, second, (zero,) * 4)
        inverse = [1.0 / jnp.sum(sums[2 * k], 0, keepdims=True) for k in both]
        inner = [jnp.sum(sums[2 * k + 1], 0, keepdims=True) * inverse[k] for k in both]

        @pl.when(g >= 1)
        def _():
            relay_z(g - 1)

        @pl.when(g >= 2)
        def _():
            relay_zy(g - 2)

        def third(c, nothing):
            at = pl.ds(pl.multiple_of(c * ROWS, ROWS), ROWS)
            for k in both:
                weight = sp_s[k, at, :TOK] * inverse[k]
                dp_s[k, at, TOK:] = weight.astype(BF)
                dp_s[k, at, :TOK] = (weight * (sp_s[k, at, TOK:] - inner[k]) * scale).astype(BF)
            return nothing

        lax.fori_loop(0, steps, third, 0)
        acc_s[...] = jnp.zeros_like(acc_s)

        def backward(p, nothing):
            at = chunk_at(p)
            key_rope = latent_chunk(p)[:, KVL:]
            for k in both:
                score_grad = dp_s[k, at, :TOK]
                rows = jnp.concatenate([kvd_s[g, at, 256 * k : 256 * k + NOPE], key_rope], 1)
                acc_s[k] += dot(score_grad, rows, TN)
                kvd_s[g, at, 256 * k : 256 * (k + 1)] = dot(dp_s[k, at, :], a_s[2 * g + k], NN).astype(BF)
            grads = jnp.concatenate([dp_s[0, at, :TOK], dp_s[1, at, :TOK]], 1)
            rope_s[at, :] += dot(grads, r_s[g], NN).astype(BF).astype(F32)
            return nothing

        lax.fori_loop(0, parts, backward, 0)
        ropes = []
        for k in both:
            chunk = acc_s[k, :, TOK:]
            ropes.append(chunk * cosine - swap_halves(chunk) * sine)
        second_nope = pltpu.roll(acc_s[1, :, :TOK], ROPE, 1)
        dg_s[g, mine] = jnp.concatenate(
            [acc_s[0, :, :TOK], jnp.where(left, ropes[0], second_nope), jnp.where(left, second_nope, ropes[1])], 1
        ).astype(BF)
        for k in (1, 2, 0):
            hand_out(g, k).start()

        @pl.when(g >= 1)
        def _():
            relay_y(g - 1)

        @pl.when(g == 2)
        def _():
            for k, (dr, dz, dy) in enumerate(TURNS):
                remote(xg_s.at[mine], xg_s.at[turn(dr, dz, dy)], sx.at[k], rx.at[k], sibling).wait_recv()

        @pl.when(g >= 2)
        def _():
            weights(g - 2)

        return carry

    lax.fori_loop(0, PAIRS, pair, 0)

    def query_out(d):
        return remote(qt_s.at[plane[d - 1]], rq_s.at[h], sqt.at[d], rqt.at[d], (r, s, plane[d - 1]))

    def send_queries():
        joined = jnp.concatenate([dg_s[g, mine] for g in range(PAIRS)], 1)
        qt_s[...] = dot(joined, wq_v[...], NT).astype(BF).reshape(HEADS, SUB, QL)
        for d in range(1, HEADS):
            query_out(d).start()


    def latent_x(p, d, source=None):
        at = column if source is None else source
        return remote(
            dl_s.at[early(p), :, beside(d)], rl_s.at[at, early(p)], sdl.at[p, d], rdl.at[p, d], in_row(d)
        )

    def latent_xy(p):
        return remote(ts_s.at[early(p), 1 - row], ry_s.at[early(p)], sdl.at[p, 0], rdl.at[p, 0], opposite)

    def latent_y(p):
        return remote(dl_s.at[late(p), 1 - row], rb_s.at[late(p)], sdl.at[p, 4], rdl.at[p, 4], opposite)

    def latent_yx(p, d, source=None):
        at = column if source is None else source
        return remote(
            tb_s.at[late(p), beside(d)], rx_s.at[at, late(p)], sdl.at[p, 4 + d], rdl.at[p, 4 + d], in_row(d)
        )

    def latents(p):
        at = chunk_at(p)
        rows = jnp.concatenate([kvd_s[g, at, :] for g in range(PAIRS)], 1)
        low_part = dot(rows, wkv_v[...], NT).astype(BF)
        rope = rope_s[at, :]
        rope = (rope + pltpu.roll(rope, ROPE, 1)).astype(BF)
        dl_s[slots_of(p)] = jnp.concatenate([low_part, rope], 1).reshape(4, 2, 4, SUB, LAT)
        latent_y(p).start()
        for d in range(1, 4):
            latent_x(p, d).start()

    def query_share(d):
        return remote(qs_s, qg_ref.at[h], sqa.at[d], rqa.at[d], (r, s, plane[d - 1]))

    def share_queries():
        total = qt_s[h].astype(F32)
        for d in range(1, HEADS):
            source = lax.rem(h - d + HEADS, HEADS)
            remote(qt_s.at[h], rq_s.at[source], sqt.at[d], rqt.at[d], (r, s, source)).wait_recv()
            total += rq_s[source].astype(F32)
        qs_s[...] = total.astype(BF)
        qg_ref[h] = qs_s[...]
        for d in range(1, HEADS):
            query_share(d).start()


    def to_latent_owner(k):
        return remote(ls_s.at[k], rlat_s.at[slot], sls.at[k], rls.at[slot], (r, base + k, h))

    def from_latent_source(k):
        return remote(ls_s.at[k], rlat_s.at[k], sls.at[k], rls.at[k], (r, base + k, h))

    def add_row(p):
        latent_y(p).wait_recv()
        for k in (4 * p + 2, 4 * p + 3):
            tb_s[k] = (dl_s[k, row].astype(F32) + rb_s[k].astype(F32)).astype(BF)
        for d in range(1, 4):
            latent_yx(p, d).start()
        for d in range(1, 4):
            latent_x(p, d, behind(d)).wait_recv()
        for k in (4 * p, 4 * p + 1):
            total = dl_s[k, :, column].astype(F32)
            for d in range(1, 4):
                total += rl_s[beside(d), k].astype(F32)
            ts_s[k] = total.astype(BF)
        latent_xy(p).start()

    def add_column(p):
        for d in range(1, 4):
            latent_yx(p, d, behind(d)).wait_recv()
        latent_xy(p).wait_recv()
        for k in range(4 * p, 4 * p + 4):
            if k % 4 < 2:
                total = ts_s[k, row].astype(F32) + ry_s[k].astype(F32)
            else:
                total = tb_s[k, column].astype(F32)
                for d in range(1, 4):
                    total += rx_s[beside(d), k].astype(F32)
            ls_s[k] = total.astype(BF)

            @pl.when(older(k))
            def _():
                to_latent_owner(k).start()

    latents(0)
    relay_z(3)
    relay_zy(2)
    pl.when(parts > 1)(lambda: latents(1))
    relay_y(3)
    weights(2)
    pl.when(parts > 2)(lambda: latents(2))
    relay_zy(3)
    weights(3)
    send_queries()
    add_row(0)
    pl.when(parts > 1)(lambda: add_row(1))
    add_column(0)
    share_queries()
    pl.when(parts > 2)(lambda: add_row(2))
    pl.when(parts > 1)(lambda: add_column(1))
    pl.when(parts > 2)(lambda: add_column(2))

    for g in range(PAIRS):
        total = wp_s[g, piece(0)].astype(F32)
        for d in range(1, REACH):
            from_source(g, d).wait_recv()
            total += rw_s[g, d].astype(F32)
        w_ref[:, 384 * g : 384 * (g + 1)] = total.astype(BF)

    acc_s[0, :SUB, :] = ls_s[slot, :, :256].astype(F32)
    acc_s[0, SUB : 2 * SUB, :] = ls_s[slot, :, 256:512].astype(F32)
    acc_s[0, 2 * SUB : 3 * SUB, :TOK] = ls_s[slot, :, 512:].astype(F32)
    for k in range(SLOTS):
        @pl.when(fresh(k))
        def _():
            from_latent_source(k).wait_recv()
            acc_s[0, :SUB, :] += rlat_s[k, :, :256].astype(F32)
            acc_s[0, SUB : 2 * SUB, :] += rlat_s[k, :, 256:512].astype(F32)
            acc_s[0, 2 * SUB : 3 * SUB, :TOK] += rlat_s[k, :, 512:].astype(F32)
    l_ref[...] = jnp.concatenate(
        [acc_s[0, :SUB, :], acc_s[0, SUB : 2 * SUB, :], acc_s[0, 2 * SUB : 3 * SUB, :ROPE]], 1
    ).astype(BF)

    for d in range(1, HEADS):
        source = lax.rem(h - d + HEADS, HEADS)
        remote(qs_s, qg_ref.at[source], sqa.at[d], rqa.at[d], (r, s, source)).wait_recv()
        query_share(d).wait_send()
        query_out(d).wait_send()
    for k in range(SLOTS):
        @pl.when(fresh(k))
        def _():
            to_seq(k).wait_send()

        @pl.when(older(k))
        def _():
            to_latent_owner(k).wait_send()
    for k in range(7):
        columns(k).wait_send()

    def drain_part(p, nothing):
        share_y(p).wait_send()
        late_xy(p).wait_send()
        for d in range(1, 4):
            share_x(p, d).wait_send()
            share_yx(p, d).wait_send()
            late_x(p, d).wait_send()
        for d in range(1, 4):
            latent_x(p, d).wait_send()
            latent_yx(p, d).wait_send()
        latent_xy(p).wait_send()
        latent_y(p).wait_send()
        return nothing

    lax.fori_loop(0, parts, drain_part, 0)

    def drain_pair(g, nothing):
        for k in range(7):
            hand_out(g, k).wait_send()
        for d in range(1, REACH):
            to_owner(g, d).wait_send()
        return nothing

    lax.fori_loop(0, PAIRS, drain_pair, 0)


def backward_pass(x, kv, wq, wkv, do, trig, positions):
    dma = pltpu.SemaphoreType.DMA
    vmem = pl.BlockSpec(memory_space=pltpu.VMEM)
    hbm = pl.BlockSpec(memory_space=pl.ANY)
    return pl.pallas_call(
        kernel,
        out_shape=(
            jax.ShapeDtypeStruct((HEADS, SUB, QL), BF),
            jax.ShapeDtypeStruct((48, QL), BF),
            jax.ShapeDtypeStruct((SUB, KVL + ROPE), BF),
        ),
        in_specs=[vmem, vmem, hbm, hbm, vmem, vmem, vmem],
        out_specs=(vmem,) * 3,
        scratch_shapes=[
            pltpu.VMEM((QL, QL), BF),
            pltpu.VMEM((KVL, 2048), BF),
            pltpu.VMEM((HEADS, SUB, LAT), BF),
            pltpu.VMEM((2, 16, 2, 48, TOK), BF),
            pltpu.VMEM((SLOTS, HEADS, SUB, LAT), BF),
            pltpu.VMEM((MEMBERS, REACH, 48, TOK), BF),
            pltpu.VMEM((HEADS, 2 * TOK, 2 * TOK), BF),
            pltpu.VMEM((PAIRS, 2 * TOK, TOK), BF),
            pltpu.VMEM((PAIRS, KEYS, 512), BF),
            pltpu.VMEM((2, KEYS, 2 * TOK), F32),
            pltpu.VMEM((KEYS, 2 * TOK), F32),
            pltpu.VMEM((2, KEYS, 2 * TOK), BF),
            pltpu.VMEM((KEYS, TOK), F32),
            pltpu.VMEM((2, TOK, 2 * TOK), F32),
            pltpu.VMEM((PAIRS, MEMBERS, TOK, 384), BF),
            pltpu.VMEM((PAIRS, REACH, 48, 384), BF),
            pltpu.VMEM((PAIRS, REACH, 48, 384), BF),
            pltpu.VMEM((HEADS, SUB, QL), BF),
            pltpu.VMEM((HEADS, SUB, QL), BF),
            pltpu.VMEM((SUB, QL), BF),
            pltpu.VMEM((SLOTS, 2, 4, SUB, LAT), BF),
            pltpu.VMEM((4, SLOTS, 2, SUB, LAT), BF),
            pltpu.VMEM((SLOTS, 2, SUB, LAT), BF),
            pltpu.VMEM((SLOTS, SUB, LAT), BF),
            pltpu.VMEM((SLOTS, 4, SUB, LAT), BF),
            pltpu.VMEM((SLOTS, 4, SUB, LAT), BF),
            pltpu.VMEM((4, SLOTS, SUB, LAT), BF),
            pltpu.VMEM((SLOTS, SUB, LAT), BF),
            pltpu.VMEM((SLOTS, SUB, LAT), BF),
            dma((2,)),
            dma((SLOTS,)), dma((SLOTS,)),
            dma((PARTS, 11)), dma((PARTS, 11)),
            dma((7,)), dma((7,)),
            dma((PAIRS, 7)), dma((PAIRS, 7)),
            dma((PAIRS, REACH)), dma((PAIRS, REACH)),
            dma((HEADS,)), dma((HEADS,)),
            dma((HEADS,)), dma((HEADS,)),
            dma((PARTS, HEADS)), dma((PARTS, HEADS)),
            dma((SLOTS,)), dma((SLOTS,)),
        ],
        compiler_params=pltpu.CompilerParams(
            collective_id=0, has_side_effects=True, vmem_limit_bytes=VMEM_LIMIT
        ),
        name="attention_backward",
    )(x, kv, wq, wkv, do, trig, positions)


def hand_over_kernel(*refs):
    for source, target in zip(refs[:3], refs[3:]):
        target[...] = source[...]


def hand_over(*arrays):
    vmem = pl.BlockSpec(memory_space=pltpu.VMEM)
    return pl.pallas_call(
        hand_over_kernel,
        out_shape=tuple(jax.ShapeDtypeStruct(a.shape, a.dtype) for a in arrays),
        in_specs=[vmem] * 3,
        out_specs=(vmem,) * 3,
        name="hand_over",
    )(*arrays)


def shards(query_latent, kv_latent, query_up, kv_up, out_grad, positions):
    s = lax.axis_index("seq")
    local_positions = lax.dynamic_slice_in_dim(positions[0], s * TOK, TOK)
    half = ROPE // 2
    lane = jnp.arange(ROPE)
    rates = 10000.0 ** (-(lane % half).astype(F32) / half)
    angles = local_positions.astype(F32)[:, None] * rates[None, :]
    trig = jnp.where(lane[None, :] < half, jnp.cos(angles), jnp.sin(angles))
    query_grad, weight_grad, latent_grad = backward_pass(
        query_latent[0], kv_latent[0].T, query_up, kv_up, out_grad[0], trig, positions
    )
    query_grad, weight_grad, latent_grad = hand_over(query_grad, weight_grad, latent_grad)
    return query_grad.reshape(1, TOK, QL), latent_grad[None], weight_grad


def solution(mesh):
    return jax.shard_map(
        shards,
        mesh=mesh,
        in_specs=(
            P("rep", "seq", None),
            P("rep", "seq", None),
            P(None, "head"),
            P(None, "head"),
            P("rep", "seq", "head"),
            P("rep", None),
        ),
        out_specs=(
            P("rep", "seq", None),
            P("rep", ("seq", "head"), None),
            P(("rep", "seq"), "head"),
        ),
        check_vma=False,
    )
```

```python
import jax
import jax.numpy as jnp
from jax import lax
from jax.experimental import pallas as pl
from jax.experimental.pallas import tpu as pltpu
from jax.sharding import PartitionSpec as P

QL = 1536
KVL = 512
ROPE = 64
NOPE = 128
VD = 128
HEADS = 8
TOK = 128
SLOTS = 12
SUB = 16
LAT = 640
KEYS = SLOTS * TOK
FIRST = 12
BF = jnp.bfloat16
F32 = jnp.float32
MESH = pl.DeviceIdType.MESH
VMEM_LIMIT = 63 * 1024 * 1024


def place():
    return lax.axis_index("rep"), lax.axis_index("seq"), lax.axis_index("head")


def group_base(s):
    return jnp.where(s < FIRST, 0, FIRST)


def z_partner(s):
    return s + 2 - 4 * lax.rem(lax.div(s, 2), 2)


def peer_rows(s):
    return lax.rem(lax.div(s, 2), 2)


def member(r, zb, yh):
    return 4 * r + 2 * zb + yh


def covered(z, zb, j):
    return lax.rem(jnp.where(zb == 0, z - j + 8, z + j), 8)


def remote(src, dst, send, recv, device):
    return pltpu.make_async_remote_copy(
        src_ref=src, dst_ref=dst, send_sem=send, recv_sem=recv, device_id=device, device_id_type=MESH
    )


def window(z, zb):
    return jnp.where(zb == 0, lax.rem(z + 5, 8), z)


def source_z(z, j):
    down = lax.rem(z + j, 8)
    up = lax.rem(z - j + 8, 8)
    return jnp.where(lax.rem(down, 2) == 0, down, up)


NT = (((1,), (1,)), ((), ()))
TN = (((0,), (0,)), ((), ()))
NN = (((1,), (0,)), ((), ()))
PAIRS = HEADS // 2
PARTS = 3
CHUNK = KEYS // PARTS
ROWS = 128


def dot(a, b, dims):
    return lax.dot_general(a, b, dims, preferred_element_type=F32)


def swap_halves(v):
    lane = lax.broadcasted_iota(jnp.int32, v.shape, 1)
    half = ROPE // 2
    return jnp.where(lax.rem(lane, ROPE) < half, pltpu.roll(v, TOK - half, 1), pltpu.roll(v, half, 1))


TURNS = [(dr, dz, dy) for dr in range(2) for dz in range(2) for dy in range(2)][1:]
MEMBERS = 8
REACH = 4


def kernel(
    x_ref, kv_ref, wq_hbm, wkv_hbm, do_ref, trig_ref, pos_ref,
    qg_ref, w_ref, l_ref,
    wq_v, wkv_v, kvx_s, xt_s, lat_s, xg_s, a_s, r_s, kvd_s, sp_s, sr_s, dp_s, rope_s, acc_s,
    dg_s, wp_s, rw_s, qt_s, rq_s, qs_s, dl_s, rl_s, ts_s, ry_s, rb_s, tb_s, rx_s, ls_s, rlat_s,
    load, s1, r1, s2, r2, sx, rx, sdq, rdq, sw, rw, sqt, rqt, sqa, rqa, sdl, rdl, sls, rls,
):
    r, s, h = place()
    big = s < FIRST
    base = group_base(s)
    slot = s - base
    members = jnp.where(big, SLOTS, 4)
    part = lax.div(slot, 4)
    parts = part + 1
    z, zb, yh = lax.div(s, 2), peer_rows(s), lax.rem(s, 2)
    other = z_partner(s)
    mine = member(r, zb, yh)
    across = lax.rem(yh + 1, 2) - yh
    sibling, partner, far = (1 - r, s, h), (r, other, h), (r, s + across, h)
    plane = [lax.rem(h + d, HEADS) for d in range(1, HEADS)]
    circle = [(lax.rem(r + dr, 2), (other if dz else s) + across * dy, h) for dr, dz, dy in TURNS]
    owners = [(r, 2 * covered(z, zb, d) + yh, h) for d in range(REACH)]
    sources = [(r, 2 * source_z(z, d) + yh, h) for d in range(REACH)]

    barrier = pltpu.get_barrier_semaphore()

    def signal(device):
        pl.semaphore_signal(barrier, inc=1, device_id=device, device_id_type=MESH)

    for peer in plane:
        signal((r, s, peer))
    for device in circle:
        signal(device)
    for device in sources[1:]:
        signal(device)
    for k in range(SLOTS):
        @pl.when((k != slot) & (k < members))
        def _():
            signal((r, base + k, h))

    loads = [
        pltpu.make_async_copy(wq_hbm, wq_v, load.at[0]),
        pltpu.make_async_copy(wkv_hbm, wkv_v, load.at[1]),
    ]
    for copy in loads:
        copy.start()
    kvx_s[...] = jnp.concatenate([kv_ref[...], kv_ref[KVL:, :]], 0).T.reshape(HEADS, SUB, LAT)
    lat_s[slot, h] = kvx_s[h]
    pl.semaphore_wait(barrier, members - 1 + 17)

    def to_seq(k):
        return remote(kvx_s.at[h], lat_s.at[slot, h], s1.at[k], r1.at[slot], (r, base + k, h))

    def from_seq(k):
        return remote(kvx_s.at[h], lat_s.at[k, h], s1.at[k], r1.at[k], (r, base + k, h))

    def fresh(k):
        return (k != slot) & (k < members) & (k // 4 >= part)

    def older(k):
        return (k != slot) & (k < members) & ((k // 4 if isinstance(k, int) else lax.div(k, 4)) <= part)

    for k in range(SLOTS):
        @pl.when(fresh(k))
        def _():
            to_seq(k).start()

    def columns(k):
        dr, dz, dy = TURNS[k]
        pr, pzb, py = lax.rem(r + dr, 2), lax.rem(zb + dz, 2), lax.rem(yh + dy, 2)
        start = window(lax.div(other if dz else s, 2), pzb)
        return remote(xt_s.at[pr, pl.ds(start, REACH), py], xg_s.at[mine], sx.at[k], rx.at[k], circle[k])

    def slots_of(p):
        return pl.ds(pl.multiple_of(4 * p, 4), 4)

    row, column = lax.div(h, 4), lax.rem(h, 4)

    def early(p):
        return pl.ds(pl.multiple_of(4 * p, 2), 2)

    def late(p):
        return pl.ds(pl.multiple_of(4 * p + 2, 2), 2)

    def beside(d):
        return lax.rem(column + d, 4)

    def in_row(d):
        return (r, s, 4 * row + beside(d))

    opposite = (r, s, 4 * (1 - row) + column)

    def behind(d):
        return lax.rem(column - d + 4, 4)

    def block(at, heads, to, p, n):
        ref = lat_s.at[at, heads]
        return remote(ref, ref, s2.at[p, n], r2.at[p, n], to)

    turned_h = 4 * (1 - row) + column

    def share_y(p, h_from=None):
        return block(early(p), h if h_from is None else h_from, opposite, p, 0)

    def share_x(p, d, h_from=None):
        return block(early(p), h if h_from is None else h_from, in_row(d), p, d)

    def share_yx(p, d, h_from=None):
        return block(early(p), turned_h if h_from is None else h_from, in_row(d), p, 3 + d)

    def late_x(p, d, h_from=None):
        return block(late(p), h if h_from is None else h_from, in_row(d), p, 6 + d)

    def late_xy(p, from_row=None):
        at = pl.ds(pl.multiple_of(4 * (row if from_row is None else from_row), 4), 4)
        return block(late(p), at, opposite, p, 10)

    scale = (NOPE + ROPE) ** (-0.5)
    cosine = jnp.concatenate([trig_ref[:, : ROPE // 2]] * 4, 1)
    sine = jnp.concatenate([-trig_ref[:, ROPE // 2 :], trig_ref[:, ROPE // 2 :]] * 2, 1)
    left = lax.broadcasted_iota(jnp.int32, (TOK, TOK), 1) < ROPE
    loads[0].wait()
    for g in range(PAIRS):
        projected = dot(x_ref[...], wq_v[:, 384 * g : 384 * (g + 1)], NN)
        one, mid, last = (projected[:, TOK * k : TOK * (k + 1)] for k in range(3))
        two = jnp.where(left, pltpu.roll(mid, ROPE, 1), pltpu.roll(last, ROPE, 1))
        none = jnp.zeros((TOK, TOK), BF)
        for k, nope in enumerate((one, two)):
            i = 2 * g + k
            a_s[i, :TOK, :TOK] = nope.astype(BF)
            a_s[i, :TOK, TOK:] = none
            a_s[i, TOK:, :TOK] = none
            a_s[i, TOK:, TOK:] = do_ref[:, TOK * i : TOK * (i + 1)]
        r_s[g, :TOK, :] = jnp.where(left, mid * cosine + swap_halves(mid) * sine, 0.0).astype(BF)
        r_s[g, TOK:, :] = jnp.where(left, 0.0, last * cosine + swap_halves(last) * sine).astype(BF)
    rope_s[...] = jnp.zeros_like(rope_s)
    def share(i, nothing):
        p = part - i
        for k in range(4):
            @pl.when(older(4 * p + k))
            def _():
                from_seq(4 * p + k).wait_recv()
        share_y(p).start()
        for d in range(1, 4):
            late_x(p, d).start()
        for d in range(1, 4):
            share_x(p, d).start()

        @pl.when(i >= 1)
        def _():
            onward(p + 1)

        return nothing

    def onward(p):
        share_y(p, turned_h).wait_recv()
        for d in range(1, 4):
            share_yx(p, d).start()
        for d in range(1, 4):
            late_x(p, d, 4 * row + behind(d)).wait_recv()
        late_xy(p).start()

    lax.fori_loop(0, parts, share, 0)
    onward(0)
    turned = x_ref[...].T.reshape(2, 8, 2, 48, TOK)
    xt_s[:, :8] = turned
    xt_s[:, 8:] = turned
    for k in range(7):
        columns(k).start()
    xg_s[mine] = xt_s[r, pl.ds(window(z, zb), REACH), yh]
    loads[1].wait()

    def chunk_at(p):
        return pl.ds(pl.multiple_of(p * CHUNK, CHUNK), CHUNK)

    def latent_chunk(p):
        return lat_s[slots_of(p)].reshape(CHUNK, LAT)

    def keys_of(i, nothing):
        p = part - i
        for d in range(1, 4):
            share_x(p, d, 4 * row + behind(d)).wait_recv()
            share_yx(p, d, 4 * (1 - row) + behind(d)).wait_recv()
        late_xy(p, 1 - row).wait_recv()
        rows = latent_chunk(p)[:, :KVL]
        for g in range(PAIRS):
            kvd_s[g, chunk_at(p), :] = dot(rows, wkv_v[:, 512 * g : 512 * (g + 1)], NN).astype(BF)
        return nothing

    lax.fori_loop(0, parts, keys_of, 0)
    first_row = pl.ds(pl.multiple_of(s * TOK, TOK), TOK)
    high = slot * TOK + lax.broadcasted_iota(jnp.int32, (1, TOK), 1)
    low = high - pos_ref[:, first_row]
    steps = parts * (CHUNK // ROWS)
    fold = (ROWS // 8, 8, TOK)
    both = range(2)

    routes = [
        (0, 0, sibling), (0, 0, partner), (0, 0, far), (1, 0, sibling), (1, 0, far), (0, 1, sibling), (1, 1, sibling)
    ]
    arrivals = [(1, 0, 0), (0, 1, 0), (0, 0, 1), (1, 1, 0), (0, 1, 1), (1, 0, 1), (1, 1, 1)]

    def turn(dr, dz, dy):
        return member(lax.rem(r + dr, 2), lax.rem(zb + dz, 2), lax.rem(yh + dy, 2))

    def hand_out(g, k):
        dz, dy, device = routes[k]
        block = dg_s.at[g, turn(0, dz, dy)]
        return remote(block, block, sdq.at[g, k], rdq.at[g, k], device)

    def hand_in(g, k):
        block = dg_s.at[g, turn(*arrivals[k])]
        return remote(block, block, sdq.at[g, k], rdq.at[g, k], sibling)

    def relay(g, arrived, onward):
        hand_in(g, arrived).wait_recv()
        for k in onward:
            hand_out(g, k).start()

    def relay_z(g):
        relay(g, 1, (4, 3))

    def relay_y(g):
        relay(g, 2, (5,))

    def relay_zy(g):
        relay(g, 4, (6,))

    def piece(d):
        return jnp.where(zb == 0, REACH - 1 - d, d)

    def to_owner(g, d):
        return remote(wp_s.at[g, piece(d)], rw_s.at[g, d], sw.at[g, d], rw.at[g, d], owners[d])

    def from_source(g, d):
        return remote(wp_s.at[g, 0], rw_s.at[g, d], sw.at[g, d], rw.at[g, d], sources[d])

    def weights(g):
        for k in (0, 3, 5, 6):
            hand_in(g, k).wait_recv()
        rows = jnp.concatenate([xg_s[k].reshape(REACH * 48, TOK) for k in range(MEMBERS)], 1)
        product = dot(rows, dg_s[g].reshape(MEMBERS * TOK, 384), NN)
        wp_s[g] = product.astype(BF).reshape(REACH, 48, 384)
        for d in (3, 2, 1):
            to_owner(g, d).start()

    def pair(g, carry):
        def scores(p, nothing):
            at = chunk_at(p)
            for k in both:
                sp_s[k, at, :] = dot(kvd_s[g, at, 256 * k : 256 * (k + 1)], a_s[2 * g + k], NT)
            sr_s[at, :] = dot(latent_chunk(p)[:, KVL:], r_s[g], NT)
            return nothing

        lax.fori_loop(0, parts, scores, 0)

        def first(c, tops):
            at = pl.ds(pl.multiple_of(c * ROWS, ROWS), ROWS)
            key = c * ROWS + lax.broadcasted_iota(jnp.int32, (ROWS, TOK), 0)
            seen = (key >= low) & (key <= high)
            out = []
            for k in both:
                value = (sp_s[k, at, :TOK] + sr_s[at, TOK * k : TOK * (k + 1)]) * scale
                value = jnp.where(seen, value, -jnp.inf)
                sp_s[k, at, :TOK] = value
                out.append(jnp.maximum(tops[k], jnp.max(value.reshape(fold), 0)))
            return tuple(out)

        start = jnp.full((8, TOK), -jnp.inf, F32)
        tops = lax.fori_loop(0, steps, first, (start, start))
        tops = [jnp.max(top, 0, keepdims=True) for top in tops]

        def second(c, sums):
            at = pl.ds(pl.multiple_of(c * ROWS, ROWS), ROWS)
            out = []
            for k in both:
                value = jnp.exp(sp_s[k, at, :TOK] - tops[k])
                sp_s[k, at, :TOK] = value
                out.append(sums[2 * k] + jnp.sum(value.reshape(fold), 0))
                out.append(sums[2 * k + 1] + jnp.sum((value * sp_s[k, at, TOK:]).reshape(fold), 0))
            return tuple(out)

        zero = jnp.zeros((8, TOK), F32)
        sums = lax.fori_loop(0, steps, second, (zero,) * 4)
        inverse = [1.0 / jnp.sum(sums[2 * k], 0, keepdims=True) for k in both]
        inner = [jnp.sum(sums[2 * k + 1], 0, keepdims=True) * inverse[k] for k in both]

        @pl.when(g >= 1)
        def _():
            relay_z(g - 1)

        @pl.when(g >= 2)
        def _():
            relay_zy(g - 2)

        def third(c, nothing):
            at = pl.ds(pl.multiple_of(c * ROWS, ROWS), ROWS)
            for k in both:
                weight = sp_s[k, at, :TOK] * inverse[k]
                dp_s[k, at, TOK:] = weight.astype(BF)
                dp_s[k, at, :TOK] = (weight * (sp_s[k, at, TOK:] - inner[k]) * scale).astype(BF)
            return nothing

        lax.fori_loop(0, steps, third, 0)
        acc_s[...] = jnp.zeros_like(acc_s)

        def backward(p, nothing):
            at = chunk_at(p)
            key_rope = latent_chunk(p)[:, KVL:]
            for k in both:
                score_grad = dp_s[k, at, :TOK]
                rows = jnp.concatenate([kvd_s[g, at, 256 * k : 256 * k + NOPE], key_rope], 1)
                acc_s[k] += dot(score_grad, rows, TN)
                kvd_s[g, at, 256 * k : 256 * (k + 1)] = dot(dp_s[k, at, :], a_s[2 * g + k], NN).astype(BF)
            grads = jnp.concatenate([dp_s[0, at, :TOK], dp_s[1, at, :TOK]], 1)
            rope_s[at, :] += dot(grads, r_s[g], NN).astype(BF).astype(F32)
            return nothing

        lax.fori_loop(0, parts, backward, 0)
        ropes = []
        for k in both:
            chunk = acc_s[k, :, TOK:]
            ropes.append(chunk * cosine - swap_halves(chunk) * sine)
        second_nope = pltpu.roll(acc_s[1, :, :TOK], ROPE, 1)
        dg_s[g, mine] = jnp.concatenate(
            [acc_s[0, :, :TOK], jnp.where(left, ropes[0], second_nope), jnp.where(left, second_nope, ropes[1])], 1
        ).astype(BF)
        for k in (1, 2, 0):
            hand_out(g, k).start()

        @pl.when(g >= 1)
        def _():
            relay_y(g - 1)

        @pl.when(g == 2)
        def _():
            for k, (dr, dz, dy) in enumerate(TURNS):
                remote(xg_s.at[mine], xg_s.at[turn(dr, dz, dy)], sx.at[k], rx.at[k], sibling).wait_recv()

        @pl.when(g >= 2)
        def _():
            weights(g - 2)

        return carry

    lax.fori_loop(0, PAIRS, pair, 0)

    def query_out(d):
        return remote(qt_s.at[plane[d - 1]], rq_s.at[h], sqt.at[d], rqt.at[d], (r, s, plane[d - 1]))

    def send_queries():
        joined = jnp.concatenate([dg_s[g, mine] for g in range(PAIRS)], 1)
        qt_s[...] = dot(joined, wq_v[...], NT).astype(BF).reshape(HEADS, SUB, QL)
        for d in range(1, HEADS):
            query_out(d).start()


    def latent_x(p, d, source=None):
        at = column if source is None else source
        return remote(
            dl_s.at[early(p), :, beside(d)], rl_s.at[at, early(p)], sdl.at[p, d], rdl.at[p, d], in_row(d)
        )

    def latent_xy(p):
        return remote(ts_s.at[early(p), 1 - row], ry_s.at[early(p)], sdl.at[p, 0], rdl.at[p, 0], opposite)

    def latent_y(p):
        return remote(dl_s.at[late(p), 1 - row], rb_s.at[late(p)], sdl.at[p, 4], rdl.at[p, 4], opposite)

    def latent_yx(p, d, source=None):
        at = column if source is None else source
        return remote(
            tb_s.at[late(p), beside(d)], rx_s.at[at, late(p)], sdl.at[p, 4 + d], rdl.at[p, 4 + d], in_row(d)
        )

    def latents(p):
        at = chunk_at(p)
        rows = jnp.concatenate([kvd_s[g, at, :] for g in range(PAIRS)], 1)
        low_part = dot(rows, wkv_v[...], NT).astype(BF)
        rope = rope_s[at, :]
        rope = (rope + pltpu.roll(rope, ROPE, 1)).astype(BF)
        dl_s[slots_of(p)] = jnp.concatenate([low_part, rope], 1).reshape(4, 2, 4, SUB, LAT)
        latent_y(p).start()
        for d in range(1, 4):
            latent_x(p, d).start()

    def query_share(d):
        return remote(qs_s, qg_ref.at[h], sqa.at[d], rqa.at[d], (r, s, plane[d - 1]))

    def share_queries():
        total = qt_s[h].astype(F32)
        for d in range(1, HEADS):
            source = lax.rem(h - d + HEADS, HEADS)
            remote(qt_s.at[h], rq_s.at[source], sqt.at[d], rqt.at[d], (r, s, source)).wait_recv()
            total += rq_s[source].astype(F32)
        qs_s[...] = total.astype(BF)
        qg_ref[h] = qs_s[...]
        for d in range(1, HEADS):
            query_share(d).start()


    def to_latent_owner(k):
        return remote(ls_s.at[k], rlat_s.at[slot], sls.at[k], rls.at[slot], (r, base + k, h))

    def from_latent_source(k):
        return remote(ls_s.at[k], rlat_s.at[k], sls.at[k], rls.at[k], (r, base + k, h))

    def add_row(p):
        latent_y(p).wait_recv()
        for k in (4 * p + 2, 4 * p + 3):
            tb_s[k] = (dl_s[k, row].astype(F32) + rb_s[k].astype(F32)).astype(BF)
        for d in range(1, 4):
            latent_yx(p, d).start()
        for d in range(1, 4):
            latent_x(p, d, behind(d)).wait_recv()
        for k in (4 * p, 4 * p + 1):
            total = dl_s[k, :, column].astype(F32)
            for d in range(1, 4):
                total += rl_s[beside(d), k].astype(F32)
            ts_s[k] = total.astype(BF)
        latent_xy(p).start()

    def add_column(p):
        for d in range(1, 4):
            latent_yx(p, d, behind(d)).wait_recv()
        latent_xy(p).wait_recv()
        for k in range(4 * p, 4 * p + 4):
            if k % 4 < 2:
                total = ts_s[k, row].astype(F32) + ry_s[k].astype(F32)
            else:
                total = tb_s[k, column].astype(F32)
                for d in range(1, 4):
                    total += rx_s[beside(d), k].astype(F32)
            ls_s[k] = total.astype(BF)

            @pl.when(older(k))
            def _():
                to_latent_owner(k).start()

    latents(0)
    relay_z(3)
    relay_zy(2)
    pl.when(parts > 1)(lambda: latents(1))
    pl.when(parts > 2)(lambda: latents(2))
    relay_y(3)
    weights(2)
    add_row(0)
    relay_zy(3)
    pl.when(parts > 1)(lambda: add_row(1))
    weights(3)
    send_queries()
    add_column(0)
    pl.when(parts > 2)(lambda: add_row(2))
    pl.when(parts > 1)(lambda: add_column(1))
    share_queries()
    pl.when(parts > 2)(lambda: add_column(2))

    for g in range(PAIRS):
        total = wp_s[g, piece(0)].astype(F32)
        for d in range(1, REACH):
            from_source(g, d).wait_recv()
            total += rw_s[g, d].astype(F32)
        w_ref[:, 384 * g : 384 * (g + 1)] = total.astype(BF)

    acc_s[0, :SUB, :] = ls_s[slot, :, :256].astype(F32)
    acc_s[0, SUB : 2 * SUB, :] = ls_s[slot, :, 256:512].astype(F32)
    acc_s[0, 2 * SUB : 3 * SUB, :TOK] = ls_s[slot, :, 512:].astype(F32)
    for k in range(SLOTS):
        @pl.when(fresh(k))
        def _():
            from_latent_source(k).wait_recv()
            acc_s[0, :SUB, :] += rlat_s[k, :, :256].astype(F32)
            acc_s[0, SUB : 2 * SUB, :] += rlat_s[k, :, 256:512].astype(F32)
            acc_s[0, 2 * SUB : 3 * SUB, :TOK] += rlat_s[k, :, 512:].astype(F32)
    l_ref[...] = jnp.concatenate(
        [acc_s[0, :SUB, :], acc_s[0, SUB : 2 * SUB, :], acc_s[0, 2 * SUB : 3 * SUB, :ROPE]], 1
    ).astype(BF)

    for d in range(1, HEADS):
        source = lax.rem(h - d + HEADS, HEADS)
        remote(qs_s, qg_ref.at[source], sqa.at[d], rqa.at[d], (r, s, source)).wait_recv()
        query_share(d).wait_send()
        query_out(d).wait_send()
    for k in range(SLOTS):
        @pl.when(fresh(k))
        def _():
            to_seq(k).wait_send()

        @pl.when(older(k))
        def _():
            to_latent_owner(k).wait_send()
    for k in range(7):
        columns(k).wait_send()

    def drain_part(p, nothing):
        share_y(p).wait_send()
        late_xy(p).wait_send()
        for d in range(1, 4):
            share_x(p, d).wait_send()
            share_yx(p, d).wait_send()
            late_x(p, d).wait_send()
        for d in range(1, 4):
            latent_x(p, d).wait_send()
            latent_yx(p, d).wait_send()
        latent_xy(p).wait_send()
        latent_y(p).wait_send()
        return nothing

    lax.fori_loop(0, parts, drain_part, 0)

    def drain_pair(g, nothing):
        for k in range(7):
            hand_out(g, k).wait_send()
        for d in range(1, REACH):
            to_owner(g, d).wait_send()
        return nothing

    lax.fori_loop(0, PAIRS, drain_pair, 0)


def backward_pass(x, kv, wq, wkv, do, trig, positions):
    dma = pltpu.SemaphoreType.DMA
    vmem = pl.BlockSpec(memory_space=pltpu.VMEM)
    hbm = pl.BlockSpec(memory_space=pl.ANY)
    return pl.pallas_call(
        kernel,
        out_shape=(
            jax.ShapeDtypeStruct((HEADS, SUB, QL), BF),
            jax.ShapeDtypeStruct((48, QL), BF),
            jax.ShapeDtypeStruct((SUB, KVL + ROPE), BF),
        ),
        in_specs=[vmem, vmem, hbm, hbm, vmem, vmem, vmem],
        out_specs=(vmem,) * 3,
        scratch_shapes=[
            pltpu.VMEM((QL, QL), BF),
            pltpu.VMEM((KVL, 2048), BF),
            pltpu.VMEM((HEADS, SUB, LAT), BF),
            pltpu.VMEM((2, 16, 2, 48, TOK), BF),
            pltpu.VMEM((SLOTS, HEADS, SUB, LAT), BF),
            pltpu.VMEM((MEMBERS, REACH, 48, TOK), BF),
            pltpu.VMEM((HEADS, 2 * TOK, 2 * TOK), BF),
            pltpu.VMEM((PAIRS, 2 * TOK, TOK), BF),
            pltpu.VMEM((PAIRS, KEYS, 512), BF),
            pltpu.VMEM((2, KEYS, 2 * TOK), F32),
            pltpu.VMEM((KEYS, 2 * TOK), F32),
            pltpu.VMEM((2, KEYS, 2 * TOK), BF),
            pltpu.VMEM((KEYS, TOK), F32),
            pltpu.VMEM((2, TOK, 2 * TOK), F32),
            pltpu.VMEM((PAIRS, MEMBERS, TOK, 384), BF),
            pltpu.VMEM((PAIRS, REACH, 48, 384), BF),
            pltpu.VMEM((PAIRS, REACH, 48, 384), BF),
            pltpu.VMEM((HEADS, SUB, QL), BF),
            pltpu.VMEM((HEADS, SUB, QL), BF),
            pltpu.VMEM((SUB, QL), BF),
            pltpu.VMEM((SLOTS, 2, 4, SUB, LAT), BF),
            pltpu.VMEM((4, SLOTS, 2, SUB, LAT), BF),
            pltpu.VMEM((SLOTS, 2, SUB, LAT), BF),
            pltpu.VMEM((SLOTS, SUB, LAT), BF),
            pltpu.VMEM((SLOTS, 4, SUB, LAT), BF),
            pltpu.VMEM((SLOTS, 4, SUB, LAT), BF),
            pltpu.VMEM((4, SLOTS, SUB, LAT), BF),
            pltpu.VMEM((SLOTS, SUB, LAT), BF),
            pltpu.VMEM((SLOTS, SUB, LAT), BF),
            dma((2,)),
            dma((SLOTS,)), dma((SLOTS,)),
            dma((PARTS, 11)), dma((PARTS, 11)),
            dma((7,)), dma((7,)),
            dma((PAIRS, 7)), dma((PAIRS, 7)),
            dma((PAIRS, REACH)), dma((PAIRS, REACH)),
            dma((HEADS,)), dma((HEADS,)),
            dma((HEADS,)), dma((HEADS,)),
            dma((PARTS, HEADS)), dma((PARTS, HEADS)),
            dma((SLOTS,)), dma((SLOTS,)),
        ],
        compiler_params=pltpu.CompilerParams(
            collective_id=0, has_side_effects=True, vmem_limit_bytes=VMEM_LIMIT
        ),
        name="attention_backward",
    )(x, kv, wq, wkv, do, trig, positions)


def hand_over_kernel(*refs):
    for source, target in zip(refs[:3], refs[3:]):
        target[...] = source[...]


def hand_over(*arrays):
    vmem = pl.BlockSpec(memory_space=pltpu.VMEM)
    return pl.pallas_call(
        hand_over_kernel,
        out_shape=tuple(jax.ShapeDtypeStruct(a.shape, a.dtype) for a in arrays),
        in_specs=[vmem] * 3,
        out_specs=(vmem,) * 3,
        name="hand_over",
    )(*arrays)


def shards(query_latent, kv_latent, query_up, kv_up, out_grad, positions):
    s = lax.axis_index("seq")
    local_positions = lax.dynamic_slice_in_dim(positions[0], s * TOK, TOK)
    half = ROPE // 2
    lane = jnp.arange(ROPE)
    rates = 10000.0 ** (-(lane % half).astype(F32) / half)
    angles = local_positions.astype(F32)[:, None] * rates[None, :]
    trig = jnp.where(lane[None, :] < half, jnp.cos(angles), jnp.sin(angles))
    query_grad, weight_grad, latent_grad = backward_pass(
        query_latent[0], kv_latent[0].T, query_up, kv_up, out_grad[0], trig, positions
    )
    query_grad, weight_grad, latent_grad = hand_over(query_grad, weight_grad, latent_grad)
    return query_grad.reshape(1, TOK, QL), latent_grad[None], weight_grad


def solution(mesh):
    return jax.shard_map(
        shards,
        mesh=mesh,
        in_specs=(
            P("rep", "seq", None),
            P("rep", "seq", None),
            P(None, "head"),
            P(None, "head"),
            P("rep", "seq", "head"),
            P("rep", None),
        ),
        out_specs=(
            P("rep", "seq", None),
            P("rep", ("seq", "head"), None),
            P(("rep", "seq"), "head"),
        ),
        check_vma=False,
    )
```

```python
import jax
import jax.numpy as jnp
from jax import lax
from jax.experimental import pallas as pl
from jax.experimental.pallas import tpu as pltpu
from jax.sharding import PartitionSpec as P

QL = 1536
KVL = 512
ROPE = 64
NOPE = 128
VD = 128
HEADS = 8
TOK = 128
SLOTS = 12
SUB = 16
LAT = 640
KEYS = SLOTS * TOK
FIRST = 12
BF = jnp.bfloat16
F32 = jnp.float32
MESH = pl.DeviceIdType.MESH
VMEM_LIMIT = 63 * 1024 * 1024


def place():
    return lax.axis_index("rep"), lax.axis_index("seq"), lax.axis_index("head")


def group_base(s):
    return jnp.where(s < FIRST, 0, FIRST)


def z_partner(s):
    return s + 2 - 4 * lax.rem(lax.div(s, 2), 2)


def peer_rows(s):
    return lax.rem(lax.div(s, 2), 2)


def member(r, zb, yh):
    return 4 * r + 2 * zb + yh


def covered(z, zb, j):
    return lax.rem(jnp.where(zb == 0, z - j + 8, z + j), 8)


def remote(src, dst, send, recv, device):
    return pltpu.make_async_remote_copy(
        src_ref=src, dst_ref=dst, send_sem=send, recv_sem=recv, device_id=device, device_id_type=MESH
    )


def window(z, zb):
    return jnp.where(zb == 0, lax.rem(z + 5, 8), z)


def source_z(z, j):
    down = lax.rem(z + j, 8)
    up = lax.rem(z - j + 8, 8)
    return jnp.where(lax.rem(down, 2) == 0, down, up)


NT = (((1,), (1,)), ((), ()))
TN = (((0,), (0,)), ((), ()))
NN = (((1,), (0,)), ((), ()))
PAIRS = HEADS // 2
PARTS = 3
CHUNK = KEYS // PARTS
ROWS = 128


def dot(a, b, dims):
    return lax.dot_general(a, b, dims, preferred_element_type=F32)


def swap_halves(v):
    lane = lax.broadcasted_iota(jnp.int32, v.shape, 1)
    half = ROPE // 2
    return jnp.where(lax.rem(lane, ROPE) < half, pltpu.roll(v, TOK - half, 1), pltpu.roll(v, half, 1))


TURNS = [(dr, dz, dy) for dr in range(2) for dz in range(2) for dy in range(2)][1:]
MEMBERS = 8
REACH = 4


def kernel(
    x_ref, kv_ref, wq_hbm, wkv_hbm, do_ref, trig_ref, pos_ref,
    qg_ref, w_ref, l_ref,
    wq_v, wkv_v, kvx_s, xt_s, lat_s, xg_s, a_s, r_s, kvd_s, sp_s, sr_s, dp_s, rope_s, acc_s,
    dg_s, wp_s, rw_s, qt_s, rq_s, qs_s, dl_s, rl_s, ts_s, ry_s, rb_s, tb_s, rx_s, ls_s, rlat_s,
    load, s1, r1, s2, r2, sx, rx, sdq, rdq, sw, rw, sqt, rqt, sqa, rqa, sdl, rdl, sls, rls,
):
    r, s, h = place()
    big = s < FIRST
    base = group_base(s)
    slot = s - base
    members = jnp.where(big, SLOTS, 4)
    part = lax.div(slot, 4)
    parts = part + 1
    z, zb, yh = lax.div(s, 2), peer_rows(s), lax.rem(s, 2)
    other = z_partner(s)
    mine = member(r, zb, yh)
    across = lax.rem(yh + 1, 2) - yh
    sibling, partner, far = (1 - r, s, h), (r, other, h), (r, s + across, h)
    plane = [lax.rem(h + d, HEADS) for d in range(1, HEADS)]
    circle = [(lax.rem(r + dr, 2), (other if dz else s) + across * dy, h) for dr, dz, dy in TURNS]
    owners = [(r, 2 * covered(z, zb, d) + yh, h) for d in range(REACH)]
    sources = [(r, 2 * source_z(z, d) + yh, h) for d in range(REACH)]

    barrier = pltpu.get_barrier_semaphore()

    def signal(device):
        pl.semaphore_signal(barrier, inc=1, device_id=device, device_id_type=MESH)

    for peer in plane:
        signal((r, s, peer))
    for device in circle:
        signal(device)
    for device in sources[1:]:
        signal(device)
    for k in range(SLOTS):
        @pl.when((k != slot) & (k < members))
        def _():
            signal((r, base + k, h))

    loads = [
        pltpu.make_async_copy(wq_hbm, wq_v, load.at[0]),
        pltpu.make_async_copy(wkv_hbm, wkv_v, load.at[1]),
    ]
    for copy in loads:
        copy.start()
    kvx_s[...] = jnp.concatenate([kv_ref[...], kv_ref[KVL:, :]], 0).T.reshape(HEADS, SUB, LAT)
    lat_s[slot, h] = kvx_s[h]
    pl.semaphore_wait(barrier, members - 1 + 17)

    def to_seq(k):
        return remote(kvx_s.at[h], lat_s.at[slot, h], s1.at[k], r1.at[slot], (r, base + k, h))

    def from_seq(k):
        return remote(kvx_s.at[h], lat_s.at[k, h], s1.at[k], r1.at[k], (r, base + k, h))

    def fresh(k):
        return (k != slot) & (k < members) & (k // 4 >= part)

    def older(k):
        return (k != slot) & (k < members) & ((k // 4 if isinstance(k, int) else lax.div(k, 4)) <= part)

    for k in range(SLOTS):
        @pl.when(fresh(k))
        def _():
            to_seq(k).start()

    def columns(k):
        dr, dz, dy = TURNS[k]
        pr, pzb, py = lax.rem(r + dr, 2), lax.rem(zb + dz, 2), lax.rem(yh + dy, 2)
        start = window(lax.div(other if dz else s, 2), pzb)
        return remote(xt_s.at[pr, pl.ds(start, REACH), py], xg_s.at[mine], sx.at[k], rx.at[k], circle[k])

    def slots_of(p):
        return pl.ds(pl.multiple_of(4 * p, 4), 4)

    row, column = lax.div(h, 4), lax.rem(h, 4)

    def early(p):
        return pl.ds(pl.multiple_of(4 * p, 2), 2)

    def late(p):
        return pl.ds(pl.multiple_of(4 * p + 2, 2), 2)

    def beside(d):
        return lax.rem(column + d, 4)

    def in_row(d):
        return (r, s, 4 * row + beside(d))

    opposite = (r, s, 4 * (1 - row) + column)

    def behind(d):
        return lax.rem(column - d + 4, 4)

    def block(at, heads, to, p, n):
        ref = lat_s.at[at, heads]
        return remote(ref, ref, s2.at[p, n], r2.at[p, n], to)

    turned_h = 4 * (1 - row) + column

    def share_y(p, h_from=None):
        return block(early(p), h if h_from is None else h_from, opposite, p, 0)

    def share_x(p, d, h_from=None):
        return block(early(p), h if h_from is None else h_from, in_row(d), p, d)

    def share_yx(p, d, h_from=None):
        return block(early(p), turned_h if h_from is None else h_from, in_row(d), p, 3 + d)

    def late_x(p, d, h_from=None):
        return block(late(p), h if h_from is None else h_from, in_row(d), p, 6 + d)

    def late_xy(p, from_row=None):
        at = pl.ds(pl.multiple_of(4 * (row if from_row is None else from_row), 4), 4)
        return block(late(p), at, opposite, p, 10)

    scale = (NOPE + ROPE) ** (-0.5)
    cosine = jnp.concatenate([trig_ref[:, : ROPE // 2]] * 4, 1)
    sine = jnp.concatenate([-trig_ref[:, ROPE // 2 :], trig_ref[:, ROPE // 2 :]] * 2, 1)
    left = lax.broadcasted_iota(jnp.int32, (TOK, TOK), 1) < ROPE
    loads[0].wait()
    for g in range(PAIRS):
        projected = dot(x_ref[...], wq_v[:, 384 * g : 384 * (g + 1)], NN)
        one, mid, last = (projected[:, TOK * k : TOK * (k + 1)] for k in range(3))
        two = jnp.where(left, pltpu.roll(mid, ROPE, 1), pltpu.roll(last, ROPE, 1))
        none = jnp.zeros((TOK, TOK), BF)
        for k, nope in enumerate((one, two)):
            i = 2 * g + k
            a_s[i, :TOK, :TOK] = nope.astype(BF)
            a_s[i, :TOK, TOK:] = none
            a_s[i, TOK:, :TOK] = none
            a_s[i, TOK:, TOK:] = do_ref[:, TOK * i : TOK * (i + 1)]
        r_s[g, :TOK, :] = jnp.where(left, mid * cosine + swap_halves(mid) * sine, 0.0).astype(BF)
        r_s[g, TOK:, :] = jnp.where(left, 0.0, last * cosine + swap_halves(last) * sine).astype(BF)
    rope_s[...] = jnp.zeros_like(rope_s)
    def share(i, nothing):
        p = part - i
        for k in range(4):
            @pl.when(older(4 * p + k))
            def _():
                from_seq(4 * p + k).wait_recv()
        share_y(p).start()
        for d in range(1, 4):
            late_x(p, d).start()
        for d in range(1, 4):
            share_x(p, d).start()

        @pl.when(i >= 1)
        def _():
            onward(p + 1)

        return nothing

    def onward(p):
        share_y(p, turned_h).wait_recv()
        for d in range(1, 4):
            share_yx(p, d).start()
        for d in range(1, 4):
            late_x(p, d, 4 * row + behind(d)).wait_recv()
        late_xy(p).start()

    lax.fori_loop(0, parts, share, 0)
    onward(0)
    turned = x_ref[...].T.reshape(2, 8, 2, 48, TOK)
    xt_s[:, :8] = turned
    xt_s[:, 8:] = turned
    for k in range(7):
        columns(k).start()
    xg_s[mine] = xt_s[r, pl.ds(window(z, zb), REACH), yh]
    loads[1].wait()

    def chunk_at(p):
        return pl.ds(pl.multiple_of(p * CHUNK, CHUNK), CHUNK)

    def latent_chunk(p):
        return lat_s[slots_of(p)].reshape(CHUNK, LAT)

    def keys_of(i, nothing):
        p = part - i
        for d in range(1, 4):
            share_x(p, d, 4 * row + behind(d)).wait_recv()
            share_yx(p, d, 4 * (1 - row) + behind(d)).wait_recv()
        late_xy(p, 1 - row).wait_recv()
        rows = latent_chunk(p)[:, :KVL]
        for g in range(PAIRS):
            kvd_s[g, chunk_at(p), :] = dot(rows, wkv_v[:, 512 * g : 512 * (g + 1)], NN).astype(BF)
        return nothing

    lax.fori_loop(0, parts, keys_of, 0)
    first_row = pl.ds(pl.multiple_of(s * TOK, TOK), TOK)
    high = slot * TOK + lax.broadcasted_iota(jnp.int32, (1, TOK), 1)
    low = high - pos_ref[:, first_row]
    steps = parts * (CHUNK // ROWS)
    fold = (ROWS // 8, 8, TOK)
    both = range(2)

    routes = [
        (0, 0, sibling), (0, 0, partner), (0, 0, far), (1, 0, sibling), (1, 0, far), (0, 1, sibling), (1, 1, sibling)
    ]
    arrivals = [(1, 0, 0), (0, 1, 0), (0, 0, 1), (1, 1, 0), (0, 1, 1), (1, 0, 1), (1, 1, 1)]

    def turn(dr, dz, dy):
        return member(lax.rem(r + dr, 2), lax.rem(zb + dz, 2), lax.rem(yh + dy, 2))

    def hand_out(g, k):
        dz, dy, device = routes[k]
        block = dg_s.at[g, turn(0, dz, dy)]
        return remote(block, block, sdq.at[g, k], rdq.at[g, k], device)

    def hand_in(g, k):
        block = dg_s.at[g, turn(*arrivals[k])]
        return remote(block, block, sdq.at[g, k], rdq.at[g, k], sibling)

    def relay(g, arrived, onward):
        hand_in(g, arrived).wait_recv()
        for k in onward:
            hand_out(g, k).start()

    def relay_z(g):
        relay(g, 1, (4, 3))

    def relay_y(g):
        relay(g, 2, (5,))

    def relay_zy(g):
        relay(g, 4, (6,))

    def piece(d):
        return jnp.where(zb == 0, REACH - 1 - d, d)

    def to_owner(g, d):
        return remote(wp_s.at[g, piece(d)], rw_s.at[g, d], sw.at[g, d], rw.at[g, d], owners[d])

    def from_source(g, d):
        return remote(wp_s.at[g, 0], rw_s.at[g, d], sw.at[g, d], rw.at[g, d], sources[d])

    def weights(g):
        for k in (0, 3, 5, 6):
            hand_in(g, k).wait_recv()
        rows = jnp.concatenate([xg_s[k].reshape(REACH * 48, TOK) for k in range(MEMBERS)], 1)
        product = dot(rows, dg_s[g].reshape(MEMBERS * TOK, 384), NN)
        wp_s[g] = product.astype(BF).reshape(REACH, 48, 384)
        for d in (3, 2, 1):
            to_owner(g, d).start()

    def pair(g, carry):
        def scores(p, nothing):
            at = chunk_at(p)
            for k in both:
                sp_s[k, at, :] = dot(kvd_s[g, at, 256 * k : 256 * (k + 1)], a_s[2 * g + k], NT)
            sr_s[at, :] = dot(latent_chunk(p)[:, KVL:], r_s[g], NT)
            return nothing

        lax.fori_loop(0, parts, scores, 0)

        def first(c, tops):
            at = pl.ds(pl.multiple_of(c * ROWS, ROWS), ROWS)
            key = c * ROWS + lax.broadcasted_iota(jnp.int32, (ROWS, TOK), 0)
            seen = (key >= low) & (key <= high)
            out = []
            for k in both:
                value = (sp_s[k, at, :TOK] + sr_s[at, TOK * k : TOK * (k + 1)]) * scale
                value = jnp.where(seen, value, -jnp.inf)
                sp_s[k, at, :TOK] = value
                out.append(jnp.maximum(tops[k], jnp.max(value.reshape(fold), 0)))
            return tuple(out)

        start = jnp.full((8, TOK), -jnp.inf, F32)
        tops = lax.fori_loop(0, steps, first, (start, start))
        tops = [jnp.max(top, 0, keepdims=True) for top in tops]

        def second(c, sums):
            at = pl.ds(pl.multiple_of(c * ROWS, ROWS), ROWS)
            out = []
            for k in both:
                value = jnp.exp(sp_s[k, at, :TOK] - tops[k])
                sp_s[k, at, :TOK] = value
                out.append(sums[2 * k] + jnp.sum(value.reshape(fold), 0))
                out.append(sums[2 * k + 1] + jnp.sum((value * sp_s[k, at, TOK:]).reshape(fold), 0))
            return tuple(out)

        zero = jnp.zeros((8, TOK), F32)
        sums = lax.fori_loop(0, steps, second, (zero,) * 4)
        inverse = [1.0 / jnp.sum(sums[2 * k], 0, keepdims=True) for k in both]
        inner = [jnp.sum(sums[2 * k + 1], 0, keepdims=True) * inverse[k] for k in both]

        @pl.when(g >= 1)
        def _():
            relay_z(g - 1)

        @pl.when(g >= 2)
        def _():
            relay_zy(g - 2)

        def third(c, nothing):
            at = pl.ds(pl.multiple_of(c * ROWS, ROWS), ROWS)
            for k in both:
                weight = sp_s[k, at, :TOK] * inverse[k]
                dp_s[k, at, TOK:] = weight.astype(BF)
                dp_s[k, at, :TOK] = (weight * (sp_s[k, at, TOK:] - inner[k]) * scale).astype(BF)
            return nothing

        lax.fori_loop(0, steps, third, 0)
        acc_s[...] = jnp.zeros_like(acc_s)

        def backward(p, nothing):
            at = chunk_at(p)
            key_rope = latent_chunk(p)[:, KVL:]
            for k in both:
                score_grad = dp_s[k, at, :TOK]
                rows = jnp.concatenate([kvd_s[g, at, 256 * k : 256 * k + NOPE], key_rope], 1)
                acc_s[k] += dot(score_grad, rows, TN)
                kvd_s[g, at, 256 * k : 256 * (k + 1)] = dot(dp_s[k, at, :], a_s[2 * g + k], NN).astype(BF)
            grads = jnp.concatenate([dp_s[0, at, :TOK], dp_s[1, at, :TOK]], 1)
            rope_s[at, :] += dot(grads, r_s[g], NN).astype(BF).astype(F32)
            return nothing

        lax.fori_loop(0, parts, backward, 0)
        ropes = []
        for k in both:
            chunk = acc_s[k, :, TOK:]
            ropes.append(chunk * cosine - swap_halves(chunk) * sine)
        second_nope = pltpu.roll(acc_s[1, :, :TOK], ROPE, 1)
        dg_s[g, mine] = jnp.concatenate(
            [acc_s[0, :, :TOK], jnp.where(left, ropes[0], second_nope), jnp.where(left, second_nope, ropes[1])], 1
        ).astype(BF)
        for k in (1, 2, 0):
            hand_out(g, k).start()

        @pl.when(g >= 1)
        def _():
            relay_y(g - 1)

        @pl.when(g == 2)
        def _():
            for k, (dr, dz, dy) in enumerate(TURNS):
                remote(xg_s.at[mine], xg_s.at[turn(dr, dz, dy)], sx.at[k], rx.at[k], sibling).wait_recv()

        @pl.when(g >= 2)
        def _():
            weights(g - 2)

        return carry

    lax.fori_loop(0, PAIRS, pair, 0)

    def query_out(d):
        return remote(qt_s.at[plane[d - 1]], rq_s.at[h], sqt.at[d], rqt.at[d], (r, s, plane[d - 1]))

    def send_queries():
        joined = jnp.concatenate([dg_s[g, mine] for g in range(PAIRS)], 1)
        qt_s[...] = dot(joined, wq_v[...], NT).astype(BF).reshape(HEADS, SUB, QL)
        for d in range(1, HEADS):
            query_out(d).start()


    def latent_x(p, d, source=None):
        at = column if source is None else source
        return remote(
            dl_s.at[early(p), :, beside(d)], rl_s.at[at, early(p)], sdl.at[p, d], rdl.at[p, d], in_row(d)
        )

    def latent_xy(p):
        return remote(ts_s.at[early(p), 1 - row], ry_s.at[early(p)], sdl.at[p, 0], rdl.at[p, 0], opposite)

    def latent_y(p):
        return remote(dl_s.at[late(p), 1 - row], rb_s.at[late(p)], sdl.at[p, 4], rdl.at[p, 4], opposite)

    def latent_yx(p, d, source=None):
        at = column if source is None else source
        return remote(
            tb_s.at[late(p), beside(d)], rx_s.at[at, late(p)], sdl.at[p, 4 + d], rdl.at[p, 4 + d], in_row(d)
        )

    def latents(p):
        at = chunk_at(p)
        rows = jnp.concatenate([kvd_s[g, at, :] for g in range(PAIRS)], 1)
        low_part = dot(rows, wkv_v[...], NT).astype(BF)
        rope = rope_s[at, :]
        rope = (rope + pltpu.roll(rope, ROPE, 1)).astype(BF)
        dl_s[slots_of(p)] = jnp.concatenate([low_part, rope], 1).reshape(4, 2, 4, SUB, LAT)
        latent_y(p).start()
        for d in range(1, 4):
            latent_x(p, d).start()

    def query_share(d):
        return remote(qs_s, qg_ref.at[h], sqa.at[d], rqa.at[d], (r, s, plane[d - 1]))

    def share_queries():
        total = qt_s[h].astype(F32)
        for d in range(1, HEADS):
            source = lax.rem(h - d + HEADS, HEADS)
            remote(qt_s.at[h], rq_s.at[source], sqt.at[d], rqt.at[d], (r, s, source)).wait_recv()
            total += rq_s[source].astype(F32)
        qs_s[...] = total.astype(BF)
        qg_ref[h] = qs_s[...]
        for d in range(1, HEADS):
            query_share(d).start()


    def to_latent_owner(k):
        return remote(ls_s.at[k], rlat_s.at[slot], sls.at[k], rls.at[slot], (r, base + k, h))

    def from_latent_source(k):
        return remote(ls_s.at[k], rlat_s.at[k], sls.at[k], rls.at[k], (r, base + k, h))

    def add_row(p):
        latent_y(p).wait_recv()
        for k in (4 * p + 2, 4 * p + 3):
            tb_s[k] = (dl_s[k, row].astype(F32) + rb_s[k].astype(F32)).astype(BF)
        for d in range(1, 4):
            latent_yx(p, d).start()
        for d in range(1, 4):
            latent_x(p, d, behind(d)).wait_recv()
        for k in (4 * p, 4 * p + 1):
            total = dl_s[k, :, column].astype(F32)
            for d in range(1, 4):
                total += rl_s[beside(d), k].astype(F32)
            ts_s[k] = total.astype(BF)
        latent_xy(p).start()

    def add_column(p):
        for d in range(1, 4):
            latent_yx(p, d, behind(d)).wait_recv()
        latent_xy(p).wait_recv()
        for k in range(4 * p, 4 * p + 4):
            if k % 4 < 2:
                total = ts_s[k, row].astype(F32) + ry_s[k].astype(F32)
            else:
                total = tb_s[k, column].astype(F32)
                for d in range(1, 4):
                    total += rx_s[beside(d), k].astype(F32)
            ls_s[k] = total.astype(BF)

            @pl.when(older(k))
            def _():
                to_latent_owner(k).start()

    latents(0)
    relay_z(3)
    pl.when(parts > 1)(lambda: latents(1))
    relay_zy(2)
    pl.when(parts > 2)(lambda: latents(2))
    relay_y(3)
    weights(2)
    add_row(0)
    relay_zy(3)
    pl.when(parts > 1)(lambda: add_row(1))
    add_column(0)
    weights(3)
    send_queries()
    pl.when(parts > 2)(lambda: add_row(2))
    pl.when(parts > 1)(lambda: add_column(1))
    share_queries()
    pl.when(parts > 2)(lambda: add_column(2))

    for g in range(PAIRS):
        total = wp_s[g, piece(0)].astype(F32)
        for d in range(1, REACH):
            from_source(g, d).wait_recv()
            total += rw_s[g, d].astype(F32)
        w_ref[:, 384 * g : 384 * (g + 1)] = total.astype(BF)

    acc_s[0, :SUB, :] = ls_s[slot, :, :256].astype(F32)
    acc_s[0, SUB : 2 * SUB, :] = ls_s[slot, :, 256:512].astype(F32)
    acc_s[0, 2 * SUB : 3 * SUB, :TOK] = ls_s[slot, :, 512:].astype(F32)
    for k in range(SLOTS):
        @pl.when(fresh(k))
        def _():
            from_latent_source(k).wait_recv()
            acc_s[0, :SUB, :] += rlat_s[k, :, :256].astype(F32)
            acc_s[0, SUB : 2 * SUB, :] += rlat_s[k, :, 256:512].astype(F32)
            acc_s[0, 2 * SUB : 3 * SUB, :TOK] += rlat_s[k, :, 512:].astype(F32)
    l_ref[...] = jnp.concatenate(
        [acc_s[0, :SUB, :], acc_s[0, SUB : 2 * SUB, :], acc_s[0, 2 * SUB : 3 * SUB, :ROPE]], 1
    ).astype(BF)

    for d in range(1, HEADS):
        source = lax.rem(h - d + HEADS, HEADS)
        remote(qs_s, qg_ref.at[source], sqa.at[d], rqa.at[d], (r, s, source)).wait_recv()
        query_share(d).wait_send()
        query_out(d).wait_send()
    for k in range(SLOTS):
        @pl.when(fresh(k))
        def _():
            to_seq(k).wait_send()

        @pl.when(older(k))
        def _():
            to_latent_owner(k).wait_send()
    for k in range(7):
        columns(k).wait_send()

    def drain_part(p, nothing):
        share_y(p).wait_send()
        late_xy(p).wait_send()
        for d in range(1, 4):
            share_x(p, d).wait_send()
            share_yx(p, d).wait_send()
            late_x(p, d).wait_send()
        for d in range(1, 4):
            latent_x(p, d).wait_send()
            latent_yx(p, d).wait_send()
        latent_xy(p).wait_send()
        latent_y(p).wait_send()
        return nothing

    lax.fori_loop(0, parts, drain_part, 0)

    def drain_pair(g, nothing):
        for k in range(7):
            hand_out(g, k).wait_send()
        for d in range(1, REACH):
            to_owner(g, d).wait_send()
        return nothing

    lax.fori_loop(0, PAIRS, drain_pair, 0)


def backward_pass(x, kv, wq, wkv, do, trig, positions):
    dma = pltpu.SemaphoreType.DMA
    vmem = pl.BlockSpec(memory_space=pltpu.VMEM)
    hbm = pl.BlockSpec(memory_space=pl.ANY)
    return pl.pallas_call(
        kernel,
        out_shape=(
            jax.ShapeDtypeStruct((HEADS, SUB, QL), BF),
            jax.ShapeDtypeStruct((48, QL), BF),
            jax.ShapeDtypeStruct((SUB, KVL + ROPE), BF),
        ),
        in_specs=[vmem, vmem, hbm, hbm, vmem, vmem, vmem],
        out_specs=(vmem,) * 3,
        scratch_shapes=[
            pltpu.VMEM((QL, QL), BF),
            pltpu.VMEM((KVL, 2048), BF),
            pltpu.VMEM((HEADS, SUB, LAT), BF),
            pltpu.VMEM((2, 16, 2, 48, TOK), BF),
            pltpu.VMEM((SLOTS, HEADS, SUB, LAT), BF),
            pltpu.VMEM((MEMBERS, REACH, 48, TOK), BF),
            pltpu.VMEM((HEADS, 2 * TOK, 2 * TOK), BF),
            pltpu.VMEM((PAIRS, 2 * TOK, TOK), BF),
            pltpu.VMEM((PAIRS, KEYS, 512), BF),
            pltpu.VMEM((2, KEYS, 2 * TOK), F32),
            pltpu.VMEM((KEYS, 2 * TOK), F32),
            pltpu.VMEM((2, KEYS, 2 * TOK), BF),
            pltpu.VMEM((KEYS, TOK), F32),
            pltpu.VMEM((2, TOK, 2 * TOK), F32),
            pltpu.VMEM((PAIRS, MEMBERS, TOK, 384), BF),
            pltpu.VMEM((PAIRS, REACH, 48, 384), BF),
            pltpu.VMEM((PAIRS, REACH, 48, 384), BF),
            pltpu.VMEM((HEADS, SUB, QL), BF),
            pltpu.VMEM((HEADS, SUB, QL), BF),
            pltpu.VMEM((SUB, QL), BF),
            pltpu.VMEM((SLOTS, 2, 4, SUB, LAT), BF),
            pltpu.VMEM((4, SLOTS, 2, SUB, LAT), BF),
            pltpu.VMEM((SLOTS, 2, SUB, LAT), BF),
            pltpu.VMEM((SLOTS, SUB, LAT), BF),
            pltpu.VMEM((SLOTS, 4, SUB, LAT), BF),
            pltpu.VMEM((SLOTS, 4, SUB, LAT), BF),
            pltpu.VMEM((4, SLOTS, SUB, LAT), BF),
            pltpu.VMEM((SLOTS, SUB, LAT), BF),
            pltpu.VMEM((SLOTS, SUB, LAT), BF),
            dma((2,)),
            dma((SLOTS,)), dma((SLOTS,)),
            dma((PARTS, 11)), dma((PARTS, 11)),
            dma((7,)), dma((7,)),
            dma((PAIRS, 7)), dma((PAIRS, 7)),
            dma((PAIRS, REACH)), dma((PAIRS, REACH)),
            dma((HEADS,)), dma((HEADS,)),
            dma((HEADS,)), dma((HEADS,)),
            dma((PARTS, HEADS)), dma((PARTS, HEADS)),
            dma((SLOTS,)), dma((SLOTS,)),
        ],
        compiler_params=pltpu.CompilerParams(
            collective_id=0, has_side_effects=True, vmem_limit_bytes=VMEM_LIMIT
        ),
        name="attention_backward",
    )(x, kv, wq, wkv, do, trig, positions)


def hand_over_kernel(*refs):
    for source, target in zip(refs[:3], refs[3:]):
        target[...] = source[...]


def hand_over(*arrays):
    vmem = pl.BlockSpec(memory_space=pltpu.VMEM)
    return pl.pallas_call(
        hand_over_kernel,
        out_shape=tuple(jax.ShapeDtypeStruct(a.shape, a.dtype) for a in arrays),
        in_specs=[vmem] * 3,
        out_specs=(vmem,) * 3,
        name="hand_over",
    )(*arrays)


def shards(query_latent, kv_latent, query_up, kv_up, out_grad, positions):
    s = lax.axis_index("seq")
    local_positions = lax.dynamic_slice_in_dim(positions[0], s * TOK, TOK)
    half = ROPE // 2
    lane = jnp.arange(ROPE)
    rates = 10000.0 ** (-(lane % half).astype(F32) / half)
    angles = local_positions.astype(F32)[:, None] * rates[None, :]
    trig = jnp.where(lane[None, :] < half, jnp.cos(angles), jnp.sin(angles))
    query_grad, weight_grad, latent_grad = backward_pass(
        query_latent[0], kv_latent[0].T, query_up, kv_up, out_grad[0], trig, positions
    )
    query_grad, weight_grad, latent_grad = hand_over(query_grad, weight_grad, latent_grad)
    return query_grad.reshape(1, TOK, QL), latent_grad[None], weight_grad


def solution(mesh):
    return jax.shard_map(
        shards,
        mesh=mesh,
        in_specs=(
            P("rep", "seq", None),
            P("rep", "seq", None),
            P(None, "head"),
            P(None, "head"),
            P("rep", "seq", "head"),
            P("rep", None),
        ),
        out_specs=(
            P("rep", "seq", None),
            P("rep", ("seq", "head"), None),
            P(("rep", "seq"), "head"),
        ),
        check_vma=False,
    )
```
